256 devices in a mesh: dp: 4 (over x), tensor: 64 (over y, z, core).
Axes of the slice: x: 4, y: 4, z: 8, core: 2. Of those that a mesh axis runs over, the one named last changes fastest.
Arguments:
- grad_out: bfloat16 [4096, 8192], P('dp', 'tensor'), may hold values from -6 to 6
- acts: bfloat16 [4096, 16384], P('dp', 'tensor'), may hold values from -6 to 6
- weight: bfloat16 [8192, 16384], P('tensor'), may hold values from -0.078125 to 0.078125
- block_mask: int32 [64, 128], replicated, may hold values from 0 to 1, as said below
Outputs:
- grad_acts: bfloat16 [4096, 16384], P('dp', 'tensor')
- grad_weight: float32 [8192, 16384], P(('dp', 'tensor'))
The draws below stay inside these ranges and needn't reach their ends.
Inputs may be any that keep to these rules, and one draw needn't show every extreme that they name: `block_mask`: kept shares differ between groups of 2 consecutive block columns, from about three twentieths to nine twentieths.
All inputs are finite; a program needn't handle non-finite values.
Results may differ from the reference program's by a relative error of at most 0.001.
Values may be sent and summed in bfloat16 or wider, within the bound.
A program may use at most 128 MiB of HBM per device.

```python
import jax
import jax.numpy as jnp
from jax import lax

D = 8192
FF = 16384
BLK = 128
TOKENS = 4096
FF_TILE = 256


def draw_block_mask(key, part):
    rows = D // BLK
    cols = FF // BLK
    per_tile = FF_TILE // BLK
    groups = cols // per_tile
    first_key, second_key = jax.random.split(jax.random.fold_in(key, 11))
    order = jax.random.permutation(first_key, groups).astype(jnp.int32)
    level = 3 + order * 7 // groups
    level = jnp.repeat(level, per_tile)
    picks = jax.random.randint(second_key, (rows, cols), 0, 20)
    return (picks < level[None, :]).astype(jnp.int32)


def steps_of(key, dims, cuts, low, top_value):
    factor_of, own = 1.0, jax.random.fold_in(key, 6)
    for dim, shards_of in cuts:
        steps = jnp.exp(jax.random.uniform(jax.random.fold_in(own, dim), (shards_of,), jnp.float32, low / len(cuts), top_value / len(cuts)))
        factor_of = factor_of * jnp.repeat(steps, dims[dim] // shards_of).reshape([-1 if axis == dim else 1 for axis in range(len(dims))])
    return factor_of


def bell_draw(key, extent, scale, limit, cuts=(), kind=jnp.bfloat16):
    values = jax.random.normal(key, extent, jnp.float32) * scale
    if len(cuts) > 0:
        values = steps_of(key, extent, cuts, -0.22, 0.18) * values
    return jnp.clip(values, min=-limit, max=limit).astype(kind)


def setup_inputs(seed: int = 0) -> dict:
    splits = jax.random.split(jax.random.key(seed), 5)
    return {
        "grad_out": bell_draw(splits[0], (TOKENS, D), 1.0, 6.0, ((0, 4), (1, 64))),
        "acts": bell_draw(splits[1], (TOKENS, FF), 1.0, 6.0, ((0, 4), (1, 64))),
        "weight": bell_draw(splits[2], (D, FF), (FF // 3) ** -0.5, 0.078125, ((0, 64),)),
        "block_mask": draw_block_mask(jax.random.fold_in(splits[4], 71), 0),
    }


def expand_mask(mask, side):
    rows, cols = mask.shape
    full = jnp.broadcast_to(mask[:, None, :, None], (rows, side, cols, side))
    return full.reshape(rows * side, cols * side)


def reference(grad_out, acts, weight, block_mask):
    full_mask = expand_mask(block_mask, BLK).astype(jnp.bfloat16)
    kept = weight * full_mask
    grad_acts = jnp.dot(grad_out.astype(jnp.float32), kept.astype(jnp.float32), preferred_element_type=jnp.float32)
    grad_acts = grad_acts.astype(jnp.bfloat16)
    product = lax.dot_general(grad_out.astype(jnp.float32), acts.astype(jnp.float32), (((0,), (0,)), ((), ())), preferred_element_type=jnp.float32)
    grad_weight = product * full_mask.astype(jnp.float32) * (1.0 / (TOKENS ** 0.5))
    return grad_acts, grad_weight
```

```python
import jax
import jax.numpy as jnp
from jax import lax
from jax.experimental import pallas as pl
from jax.experimental.pallas import tpu as pltpu
from jax.sharding import PartitionSpec as P

NX, NY, NZ = 4, 4, 8
BLK = 128
BF, F32 = jnp.bfloat16, jnp.float32
MESH = pl.DeviceIdType.MESH


def kernel(go, acts, weight, mask, ga, gw, G, A, At, K, part, R, S,
           t_send, a_send, w_send, z_send, y_send, b_send, s_send, r_send,
           t_recv, a_recv, w_recv, z_recv, yp_recv, ym_recv, y2_recv, b_recv, s_recv, r_recv):
    x = lax.axis_index("dp")
    t = lax.axis_index("tensor")
    y, z, c = t // (2 * NZ), (t % (2 * NZ)) // 2, t % 2
    mine = pl.ds(pl.multiple_of(c * BLK, BLK), BLK)
    other = pl.ds(pl.multiple_of((1 - c) * BLK, BLK), BLK)
    columns = pl.ds(pl.multiple_of(t * 2 * BLK, 2 * BLK), 2 * BLK)
    tokens = go.shape[0]
    half = tokens // 2
    mate = y * 2 * NZ + z * 2 + (1 - c)
    up = ((y + 1) % NY) * 2 * NZ + z * 2 + c
    down = ((y + NY - 1) % NY) * 2 * NZ + z * 2 + c
    right = y * 2 * NZ + ((z + 1) % NZ) * 2 + c
    left = y * 2 * NZ + ((z + NZ - 1) % NZ) * 2 + c

    def send(src, dst, send_sem, recv_sem, to_x, to_t):
        pltpu.make_async_remote_copy(
            src_ref=src, dst_ref=dst, send_sem=send_sem, recv_sem=recv_sem,
            device_id=(to_x, to_t), device_id_type=MESH,
        ).start()

    def wait(region, sem):
        pltpu.make_async_copy(region, region, sem).wait()

    home = G.at[x, z, :, mine]

    @pl.when(x != y)
    def _():
        send(go, home, t_send, t_recv, y, x * 2 * NZ + z * 2 + c)

    @pl.when(x == y)
    def _():
        pltpu.make_async_copy(go, home, t_recv).start()

    pltpu.make_async_copy(acts, A.at[x], a_recv).start()
    for step in (1, 3, 2):
        send(acts, A.at[x], a_send, a_recv, (x + step) % NX, t)

    @pl.loop(0, 2 * NZ)
    def _(n):
        to_t = x * 2 * NZ + n
        src = weight.at[:, pl.ds(pl.multiple_of(to_t * 2 * BLK, 2 * BLK), 2 * BLK)]
        dst = K.at[2 * z + c]
        same = (x == y) & (n == 2 * z + c)

        @pl.when(same)
        def _():
            pltpu.make_async_copy(src, dst, w_recv).start()

        @pl.when(jnp.logical_not(same))
        def _():
            send(src, dst, w_send, w_recv, y, to_t)

    def chunk(k):
        return (z + NZ + ((k + 1) // 2) * (1 - 2 * (k % 2))) % NZ

    def stage_z(k):
        zc = chunk(k)
        block = G.at[y, zc, :, mine]

        @pl.when(k == 0)
        def _():
            wait(block, t_recv)

        @pl.when(k > 0)
        def _():
            wait(block, z_recv.at[k])

        @pl.when((k == 0) | ((k % 2 == 1) & (k < 7)))
        def _():
            send(block, block, z_send, z_recv.at[jnp.where(k == 0, 1, k + 2)], x, right)

        @pl.when((k % 2 == 0) & (k < 6))
        def _():
            send(block, block, z_send, z_recv.at[k + 2], x, left)

        send(block, block, y_send, yp_recv.at[k], x, up)
        send(block, block, y_send, ym_recv.at[k], x, down)
        send(block, block, b_send, b_recv.at[k], x, mate)

    def stage_y(k):
        zc = chunk(k)
        below, above = (y + NY - 1) % NY, (y + 1) % NY
        block = G.at[below, zc, :, mine]
        wait(block, yp_recv.at[k])
        piece = G.at[below, zc, pl.ds(0, half), mine]
        send(piece, piece, y_send, y2_recv.at[k], x, up)
        send(block, block, b_send, b_recv.at[k], x, mate)
        block = G.at[above, zc, :, mine]
        wait(block, ym_recv.at[k])
        piece = G.at[above, zc, pl.ds(half, half), mine]
        send(piece, piece, y_send, y2_recv.at[k], x, down)
        send(block, block, b_send, b_recv.at[k], x, mate)

    def stage_far(k):
        block = G.at[(y + 2) % NY, chunk(k), :, mine]
        wait(block, y2_recv.at[k])
        send(block, block, b_send, b_recv.at[k], x, mate)

    def scalar(row, h):
        return mask[x * 2 * NZ + row, 2 * t + h].astype(F32)

    scale_factor = 1.0 / (tokens * NX) ** 0.5

    def stage_weight_grad(k):
        zc = chunk(k)
        wait(G.at[:, zc, :, other], b_recv.at[k])
        total = jnp.dot(At[0], G[0, zc], preferred_element_type=F32)
        for d in range(1, NX):
            total += jnp.dot(At[d], G[d, zc], preferred_element_type=F32)
        total = total.T * scale_factor
        for r in range(2):
            for h in range(2):
                tile = total[r * BLK:(r + 1) * BLK, h * BLK:(h + 1) * BLK] * scalar(2 * zc + r, h)
                S[pl.ds(8 * zc + 4 * r, 4), :, h * BLK:(h + 1) * BLK] = tile.reshape(4, BLK // 4, BLK)

        @pl.loop(0, 8)
        def _(j):
            n = 8 * zc + j

            @pl.when(n == t)
            def _():
                pltpu.make_async_copy(S.at[n], gw.at[:, columns], s_recv).start()

            @pl.when(n != t)
            def _():
                send(S.at[n], gw.at[:, columns], s_send, s_recv, x, n)

    @pl.loop(0, NZ + 4)
    def _(i):
        @pl.when(i < NZ)
        def _():
            stage_z(i)

        @pl.when((i >= 2) & (i < NZ + 2))
        def _():
            stage_y(i - 2)

        @pl.when((i >= 3) & (i < NZ + 3))
        def _():
            stage_far(i - 3)

        @pl.when(i == 4)
        def _():
            wait(A, a_recv)
            for d in range(NX):
                At[d] = A[d].T

        @pl.when(i >= 4)
        def _():
            stage_weight_grad(i - 4)

    wait(K, w_recv)

    @pl.loop(0, 2 * NZ)
    def _(f):
        for h in range(2):
            cols = slice(h * BLK, (h + 1) * BLK)
            K[f, :, cols] = (K[f, :, cols].astype(F32) * scalar(f, h)).astype(BF)

    @pl.loop(0, NX)
    def _(rel):
        d = (y + rel) % NX

        @pl.loop(0, 4)
        def _(r):
            rows = pl.ds(pl.multiple_of(r * (tokens // 4), tokens // 4), tokens // 4)
            total = jnp.dot(G[d, 0, rows], K[0:2].reshape(2 * BLK, 2 * BLK), preferred_element_type=F32)
            for f in range(1, NZ):
                total += jnp.dot(G[d, f, rows], K[2 * f:2 * f + 2].reshape(2 * BLK, 2 * BLK),
                                 preferred_element_type=F32)
            part[d, rows] = total

        @pl.when(d != x)
        def _():
            send(part.at[d], R.at[(x + NX - d) % NX - 1], r_send, r_recv, d, t)

    wait(R, r_recv)

    @pl.loop(0, 8)
    def _(r):
        rows = pl.ds(pl.multiple_of(r * (tokens // 8), tokens // 8), tokens // 8)
        ga[rows] = ((part[x, rows] + R[0, rows]) + (R[1, rows] + R[2, rows])).astype(BF)

    wait(gw, s_recv)

    @pl.when(x != y)
    def _():
        wait(go, t_send)
        wait(K, w_send)

    @pl.when(x == y)
    def _():
        wait(K.at[pl.ds(0, 2 * NZ - 1)], w_send)

    wait(A.at[pl.ds(0, 3)], a_send)
    wait(G.at[0, pl.ds(0, 7), :, pl.ds(0, BLK)], z_send)
    wait(G.at[pl.ds(0, 3), pl.ds(0, 4)], y_send)
    wait(G.at[pl.ds(0, 2)], b_send)
    wait(S.at[pl.ds(0, 63)], s_send)
    wait(R, r_send)


def body(grad_out, acts, weight, block_mask):
    tokens, d_tile = grad_out.shape
    ff_tile = acts.shape[1]
    full_width = weight.shape[1]
    dma = pltpu.SemaphoreType.DMA
    return pl.pallas_call(
        kernel,
        out_shape=(
            jax.ShapeDtypeStruct((tokens, ff_tile), BF),
            jax.ShapeDtypeStruct((d_tile // NX, full_width), F32),
        ),
        in_specs=[pl.BlockSpec(memory_space=pl.ANY)] * 3 + [pl.BlockSpec(memory_space=pltpu.SMEM)],
        out_specs=(pl.BlockSpec(memory_space=pltpu.VMEM), pl.BlockSpec(memory_space=pl.ANY)),
        scratch_shapes=[
            pltpu.VMEM((NX, NZ, tokens, 2 * BLK), BF),
            pltpu.VMEM((NX, tokens, ff_tile), BF),
            pltpu.VMEM((NX, ff_tile, tokens), BF),
            pltpu.VMEM((2 * NZ, BLK, ff_tile), BF),
            pltpu.VMEM((NX, tokens, ff_tile), F32),
            pltpu.VMEM((NX - 1, tokens, ff_tile), F32),
            pltpu.VMEM((8 * NZ, BLK // NX, ff_tile), F32),
        ] + [dma] * 8 + [dma] * 3 + [dma((NZ,))] * 5 + [dma] * 2,
        compiler_params=pltpu.CompilerParams(
            has_side_effects=True, vmem_limit_bytes=52 * 1024 * 1024
        ),
    )(grad_out, acts, weight, block_mask)


def solution(mesh):
    in_specs = (P("dp", "tensor"), P("dp", "tensor"), P("tensor", None), P())
    out_specs = (P("dp", "tensor"), P(("dp", "tensor"), None))
    return jax.shard_map(body, mesh=mesh, in_specs=in_specs, out_specs=out_specs, check_vma=False)
```

```python
import jax
import jax.numpy as jnp
from jax import lax
from jax.experimental import pallas as pl
from jax.experimental.pallas import tpu as pltpu
from jax.sharding import PartitionSpec as P

NX, NY, NZ = 4, 4, 8
VSTART, VPASS = 1, 5
LEAD, SLICES = 7, 4
BLK = 128
BF, F32 = jnp.bfloat16, jnp.float32
MESH = pl.DeviceIdType.MESH


def kernel(go, acts, weight, mask, ga, gw, G, A, At, V, K, part, H, R, S,
           t_send, a_send, v_send, w_send, z_send, y_send, b_send, s_send, r_send,
           t_recv, a_recv, v_recv, w_recv, z_recv, yp_recv, ym_recv, y2_recv,
           yq_recv, yn_recv, y3_recv, b_recv, b2_recv, s_recv, h_recv, r_recv):
    x = lax.axis_index("dp")
    t = lax.axis_index("tensor")
    y, z, c = t // (2 * NZ), (t % (2 * NZ)) // 2, t % 2
    mine = pl.ds(pl.multiple_of(c * BLK, BLK), BLK)
    other = pl.ds(pl.multiple_of((1 - c) * BLK, BLK), BLK)
    columns = pl.ds(pl.multiple_of(t * 2 * BLK, 2 * BLK), 2 * BLK)
    tokens = go.shape[0]
    half = tokens // 2
    low, high = pl.ds(0, half), pl.ds(half, half)
    mate = y * 2 * NZ + z * 2 + (1 - c)
    up = ((y + 1) % NY) * 2 * NZ + z * 2 + c
    down = ((y + NY - 1) % NY) * 2 * NZ + z * 2 + c
    right = y * 2 * NZ + ((z + 1) % NZ) * 2 + c
    left = y * 2 * NZ + ((z + NZ - 1) % NZ) * 2 + c

    def send(src, dst, send_sem, recv_sem, to_x, to_t):
        pltpu.make_async_remote_copy(
            src_ref=src, dst_ref=dst, send_sem=send_sem, recv_sem=recv_sem,
            device_id=(to_x, to_t), device_id_type=MESH,
        ).start()

    def wait(region, sem):
        pltpu.make_async_copy(region, region, sem).wait()

    def scalar(row, h):
        return mask[x * 2 * NZ + row, 2 * t + h].astype(F32)

    barrier = pltpu.get_barrier_semaphore()
    partner = x * 2 * NZ + z * 2 + c

    @pl.loop(0, NY * 2 * NZ)
    def _(n):
        @pl.when(n != t)
        def _():
            pl.semaphore_signal(barrier, inc=1, device_id=(x, n), device_id_type=MESH)

    @pl.loop(1, NX)
    def _(step):
        @pl.loop(0, 2 * NZ)
        def _(n):
            pl.semaphore_signal(barrier, inc=1, device_id=((x + step) % NX, y * 2 * NZ + n), device_id_type=MESH)

    @pl.when(x != y)
    def _():
        pl.semaphore_signal(barrier, inc=1, device_id=(y, partner), device_id_type=MESH)

    greeted = NY * 2 * NZ - 1 + (NX - 1) * 2 * NZ

    @pl.when(x != y)
    def _():
        pl.semaphore_wait(barrier, greeted + 1)

    @pl.when(x == y)
    def _():
        pl.semaphore_wait(barrier, greeted)

    home = G.at[x, 0, :, mine]

    @pl.when(x != y)
    def _():
        send(go, home, t_send, t_recv, y, x * 2 * NZ + z * 2 + c)

    @pl.when(x == y)
    def _():
        pltpu.make_async_copy(go, home, t_recv).start()

    east, west = (x + 1) % NX, (x + NX - 1) % NX
    pltpu.make_async_copy(acts, A.at[x], a_recv.at[0]).start()

    def start_acts():
        send(acts, A.at[x], a_send, a_recv.at[1], east, t)
        send(acts, A.at[x], a_send, a_recv.at[2], west, t)

    def pass_acts():
        wait(A.at[west], a_recv.at[1])
        piece = A.at[west, pl.ds(0, half)]
        send(piece, piece, a_send, a_recv.at[3], east, t)
        wait(A.at[east], a_recv.at[2])
        piece = A.at[east, pl.ds(half, half)]
        send(piece, piece, a_send, a_recv.at[3], west, t)

    def finish_acts():
        wait(A.at[x], a_recv.at[0])
        wait(A.at[(x + 2) % NX], a_recv.at[3])
        for d in range(NX):
            At[d] = A[d].T

    quarter = BLK // NX
    wide = V.shape[2]
    strip = weight.at[pl.ds(pl.multiple_of(x * quarter, quarter), quarter)]

    def start_weights():
        for step in range(NY):
            there = (y + step) % NY
            src = strip.at[:, pl.ds(pl.multiple_of(there * wide, wide), wide)]
            if step == 0:
                pltpu.make_async_copy(src, V.at[y], v_recv).start()
            else:
                send(src, V.at[y], v_send, v_recv, x, there * 2 * NZ + 2 * z + c)

    def pass_weights():
        wait(V, v_recv)
        dst = K.at[pl.ds(pl.multiple_of(BLK * (2 * z + c) + quarter * x, quarter), quarter)]

        @pl.loop(0, NX * 2 * NZ)
        def _(m):
            e, n = m // (2 * NZ), m % (2 * NZ)
            src = V.at[e, :, pl.ds(pl.multiple_of(n * 2 * BLK, 2 * BLK), 2 * BLK)]
            same = (e == x) & (n == 2 * z + c)

            @pl.when(same)
            def _():
                pltpu.make_async_copy(src, dst, w_recv).start()

            @pl.when(jnp.logical_not(same))
            def _():
                send(src, dst, w_send, w_recv, e, y * 2 * NZ + n)

    def finish_weights():
        wait(K, w_recv)

        @pl.loop(0, 2 * NZ)
        def _(f):
            rows = pl.ds(pl.multiple_of(f * BLK, BLK), BLK)
            for h in range(2):
                cols = slice(h * BLK, (h + 1) * BLK)
                K[rows, cols] = (K[rows, cols].astype(F32) * scalar(f, h)).astype(BF)

    def chunk(k):
        return (z + NZ + ((k + 1) // 2) * (1 - 2 * (k % 2))) % NZ

    def stage_z(k):
        block = G.at[y, k, :, mine]

        @pl.when(k == 0)
        def _():
            wait(block, t_recv)

        @pl.when(k > 0)
        def _():
            wait(block, z_recv.at[k])

        @pl.when((k == 0) | ((k % 2 == 1) & (k < 7)))
        def _():
            to_k = jnp.where(k == 0, 1, k + 2)
            send(block, G.at[y, to_k, :, mine], z_send, z_recv.at[to_k], x, right)

        @pl.when((k % 2 == 0) & (k < 6))
        def _():
            send(block, G.at[y, k + 2, :, mine], z_send, z_recv.at[k + 2], x, left)

        @pl.when(k < LEAD)
        def _():
            send(block, block, y_send, yp_recv.at[k], x, up)
            send(block, block, y_send, ym_recv.at[k], x, down)

        send(block, block, b_send, b_recv.at[0, k], x, mate)

    below, above, beyond = (y + NY - 1) % NY, (y + 1) % NY, (y + 2) % NY

    def stage_y(k):
        block = G.at[below, k, :, mine]
        wait(block, yp_recv.at[k])
        piece = G.at[below, k, low, mine]
        send(piece, piece, y_send, y2_recv.at[k], x, up)
        send(block, block, b_send, b_recv.at[1, k], x, mate)
        block = G.at[above, k, :, mine]
        wait(block, ym_recv.at[k])
        piece = G.at[above, k, high, mine]
        send(piece, piece, y_send, y2_recv.at[k], x, down)
        send(block, block, b_send, b_recv.at[2, k], x, mate)

    def stage_far(k):
        block = G.at[beyond, k, :, mine]
        wait(block, y2_recv.at[k])
        send(block, block, b_send, b_recv.at[3, k], x, mate)

    late = pl.ds(LEAD, NZ - LEAD)
    size = tokens // SLICES

    def rows_of(j, part_of=None):
        if part_of is None:
            return pl.ds(pl.multiple_of(j * size, size), size)
        return pl.ds(pl.multiple_of(j * size + part_of * (size // 2), size // 2), size // 2)

    def slice_start(j):
        block = G.at[y, late, rows_of(j), mine]
        send(block, block, y_send, yq_recv.at[j], x, up)
        send(block, block, y_send, yn_recv.at[j], x, down)

    def slice_y(j):
        block = G.at[below, late, rows_of(j), mine]
        wait(block, yq_recv.at[j])
        piece = G.at[below, late, rows_of(j, 0), mine]
        send(piece, piece, y_send, y3_recv.at[j], x, up)
        send(block, block, b_send, b2_recv.at[0, j], x, mate)
        block = G.at[above, late, rows_of(j), mine]
        wait(block, yn_recv.at[j])
        piece = G.at[above, late, rows_of(j, 1), mine]
        send(piece, piece, y_send, y3_recv.at[j], x, down)
        send(block, block, b_send, b2_recv.at[1, j], x, mate)

    def slice_far(j):
        block = G.at[beyond, late, rows_of(j), mine]
        wait(block, y3_recv.at[j])
        send(block, block, b_send, b2_recv.at[2, j], x, mate)

    def slice_input_grad(j):
        for kind, d in enumerate((below, above, beyond)):
            wait(G.at[d, late, rows_of(j), other], b2_recv.at[kind, j])

        @pl.loop(0, NX)
        def _(rel):
            d = (x + 2 + rel) % NX
            rows = rows_of(j)
            total = jnp.zeros((size, 2 * BLK), F32)
            for k in range(NZ):
                kept = K[pl.ds(pl.multiple_of(2 * BLK * chunk(k), 2 * BLK), 2 * BLK)]
                total += jnp.dot(G[d, k, rows], kept, preferred_element_type=F32)
            part[d, rows] = total

            @pl.when(rel == 0)
            def _():
                send(part.at[d, rows_of(j, 0)], H.at[0, j], r_send, h_recv.at[0, j], east, t)
                send(part.at[d, rows_of(j, 1)], H.at[1, j], r_send, h_recv.at[1, j], west, t)

            @pl.when(rel == 1)
            def _():
                send(part.at[d, rows_of(j, 0)], R.at[1, rows_of(j, 0)], r_send, r_recv.at[j], west, t)

            @pl.when(rel == 3)
            def _():
                send(part.at[d, rows_of(j, 1)], R.at[0, rows_of(j, 1)], r_send, r_recv.at[j], east, t)

    def slice_pass(j):
        wait(H.at[0, j], h_recv.at[0, j])
        part[east, rows_of(j, 0)] += H[0, j]
        send(part.at[east, rows_of(j, 0)], R.at[0, rows_of(j, 0)], r_send, r_recv.at[j], east, t)
        wait(H.at[1, j], h_recv.at[1, j])
        part[west, rows_of(j, 1)] += H[1, j]
        send(part.at[west, rows_of(j, 1)], R.at[1, rows_of(j, 1)], r_send, r_recv.at[j], west, t)

    def slice_finish(j):
        wait(R.at[:, rows_of(j)], r_recv.at[j])
        rows = rows_of(j)
        ga[rows] = (part[x, rows] + R[0, rows] + R[1, rows]).astype(BF)

    scale_factor = 1.0 / (tokens * NX) ** 0.5

    def stage_weight_grad(k):
        zc = chunk(k)

        @pl.when(k < LEAD)
        def _():
            for kind, d in enumerate((y, below, above, beyond)):
                wait(G.at[d, k, :, other], b_recv.at[kind, k])

        total = jnp.dot(At[0], G[0, k], preferred_element_type=F32)
        for d in range(1, NX):
            total += jnp.dot(At[d], G[d, k], preferred_element_type=F32)
        total = total.T * scale_factor
        for r in range(2):
            for h in range(2):
                tile = total[r * BLK:(r + 1) * BLK, h * BLK:(h + 1) * BLK] * scalar(2 * zc + r, h)
                S[pl.ds(8 * zc + 4 * r, 4), :, h * BLK:(h + 1) * BLK] = tile.reshape(4, BLK // 4, BLK)

        @pl.loop(0, 8)
        def _(j):
            n = 8 * zc + j

            @pl.when(n == t)
            def _():
                pltpu.make_async_copy(S.at[n], gw.at[:, columns], s_recv).start()

            @pl.when(n != t)
            def _():
                send(S.at[n], gw.at[:, columns], s_send, s_recv, x, n)

    @pl.loop(0, LEAD + 4)
    def _(i):
        @pl.when(i < NZ)
        def _():
            stage_z(i)

        @pl.when((i >= 2) & (i < LEAD + 2))
        def _():
            stage_y(i - 2)

        @pl.when(i == LEAD + 2)
        def _():
            pl.loop(0, SLICES)(slice_start)

        @pl.when((i >= 3) & (i < LEAD + 3))
        def _():
            stage_far(i - 3)

        @pl.when(i == 0)
        def _():
            start_acts()

        @pl.when(i == VSTART)
        def _():
            start_weights()

        @pl.when(i == 3)
        def _():
            pass_acts()

        @pl.when(i == VPASS)
        def _():
            pass_weights()

        @pl.when(i == 4)
        def _():
            finish_acts()

        @pl.when(i >= 4)
        def _():
            stage_weight_grad(i - 4)

    finish_weights()

    @pl.loop(LEAD, NZ)
    def _(k):
        wait(G.at[y, k, :, other], b_recv.at[0, k])

    @pl.loop(0, SLICES + 2)
    def _(i):
        @pl.when(i < SLICES)
        def _():
            slice_y(i)

        @pl.when((i >= 1) & (i < SLICES + 1))
        def _():
            slice_far(i - 1)

        @pl.when((i >= 2) & (i < SLICES + 2))
        def _():
            slice_input_grad(i - 2)

        @pl.when((i >= 3) & (i < SLICES + 2))
        def _():
            slice_pass(i - 3)

        @pl.when(i == SLICES + 1)
        def _():
            pl.loop(LEAD, NZ)(stage_weight_grad)

    slice_pass(SLICES - 1)
    pl.loop(0, SLICES)(slice_finish)
    wait(gw, s_recv)

    @pl.when(x != y)
    def _():
        wait(go, t_send)

    wait(V.at[pl.ds(0, 3)], v_send)
    wait(K.at[pl.ds(0, 63 * quarter)], w_send)

    wait(A.at[pl.ds(0, 3)], a_send)
    wait(G.at[0, pl.ds(0, 7), :, pl.ds(0, BLK)], z_send)
    wait(G.at[pl.ds(0, 3), pl.ds(0, 4)], y_send)
    wait(G.at[pl.ds(0, 2)], b_send)
    wait(S.at[pl.ds(0, 63)], s_send)
    wait(part.at[pl.ds(0, 3)], r_send)


def body(grad_out, acts, weight, block_mask):
    tokens, d_tile = grad_out.shape
    ff_tile = acts.shape[1]
    full_width = weight.shape[1]
    dma = pltpu.SemaphoreType.DMA
    return pl.pallas_call(
        kernel,
        out_shape=(
            jax.ShapeDtypeStruct((tokens, ff_tile), BF),
            jax.ShapeDtypeStruct((d_tile // NX, full_width), F32),
        ),
        in_specs=[pl.BlockSpec(memory_space=pltpu.HBM)] * 3 + [pl.BlockSpec(memory_space=pltpu.SMEM)],
        out_specs=(pl.BlockSpec(memory_space=pltpu.VMEM), pl.BlockSpec(memory_space=pl.ANY)),
        scratch_shapes=[
            pltpu.VMEM((NX, NZ, tokens, 2 * BLK), BF),
            pltpu.VMEM((NX, tokens, ff_tile), BF),
            pltpu.VMEM((NX, ff_tile, tokens), BF),
            pltpu.VMEM((NY, d_tile // NX, full_width // NY), BF),
            pltpu.VMEM((2 * NZ * BLK, ff_tile), BF),
            pltpu.VMEM((NX, tokens, ff_tile), F32),
            pltpu.VMEM((2, SLICES, tokens // SLICES // 2, ff_tile), F32),
            pltpu.VMEM((2, tokens, ff_tile), F32),
            pltpu.VMEM((8 * NZ, BLK // NX, ff_tile), F32),
        ] + [dma] * 9 + [dma, dma((4,)), dma, dma] + [dma((NZ,))] + [dma((LEAD,))] * 3 + [dma((SLICES,))] * 3
        + [dma((4, NZ)), dma((3, SLICES)), dma, dma((2, SLICES)), dma((SLICES,))],
        compiler_params=pltpu.CompilerParams(
            collective_id=0, has_side_effects=True, vmem_limit_bytes=63 * 1024 * 1024
        ),
    )(grad_out, acts, weight, block_mask)


def solution(mesh):
    in_specs = (P("dp", "tensor"), P("dp", "tensor"), P("tensor", None), P())
    out_specs = (P("dp", "tensor"), P(("dp", "tensor"), None))
    return jax.shard_map(body, mesh=mesh, in_specs=in_specs, out_specs=out_specs, check_vma=False)
```

```python
import jax
import jax.numpy as jnp
from jax import lax
from jax.experimental import pallas as pl
from jax.experimental.pallas import tpu as pltpu
from jax.sharding import PartitionSpec as P

NX, NY, NZ = 4, 4, 8
VSTART, VPASS = 0, 5
LEAD, SLICES = 6, 4
BLK = 128
BF, F32 = jnp.bfloat16, jnp.float32
STEPS = 32767.0
MESH = pl.DeviceIdType.MESH


def kernel(go, acts, weight, mask, own, R, gw, gm, G, A, At, V, K, part, H, S, M,
           t_send, a_send, v_send, w_send, z_send, y_send, b_send, s_send, m_send, r_send,
           t_recv, a_recv, v_recv, w_recv, z_recv, yp_recv, ym_recv, y2_recv,
           yq_recv, yn_recv, y3_recv, b_recv, b2_recv, s_recv, m_recv, h_recv, r_recv, o_recv):
    x = lax.axis_index("dp")
    t = lax.axis_index("tensor")
    y, z, c = t // (2 * NZ), (t % (2 * NZ)) // 2, t % 2
    mine = pl.ds(pl.multiple_of(c * BLK, BLK), BLK)
    other = pl.ds(pl.multiple_of((1 - c) * BLK, BLK), BLK)
    columns = pl.ds(pl.multiple_of(t * 2 * BLK, 2 * BLK), 2 * BLK)
    tokens = go.shape[0]
    half = tokens // 2
    low, high = pl.ds(0, half), pl.ds(half, half)
    mate = y * 2 * NZ + z * 2 + (1 - c)
    up = ((y + 1) % NY) * 2 * NZ + z * 2 + c
    down = ((y + NY - 1) % NY) * 2 * NZ + z * 2 + c
    right = y * 2 * NZ + ((z + 1) % NZ) * 2 + c
    left = y * 2 * NZ + ((z + NZ - 1) % NZ) * 2 + c

    def send(src, dst, send_sem, recv_sem, to_x, to_t):
        pltpu.make_async_remote_copy(
            src_ref=src, dst_ref=dst, send_sem=send_sem, recv_sem=recv_sem,
            device_id=(to_x, to_t), device_id_type=MESH,
        ).start()

    def wait(region, sem):
        pltpu.make_async_copy(region, region, sem).wait()

    def scalar(row, h):
        return mask[x * 2 * NZ + row, 2 * t + h].astype(F32)

    barrier = pltpu.get_barrier_semaphore()
    partner = x * 2 * NZ + z * 2 + c

    @pl.loop(0, NY * 2 * NZ)
    def _(n):
        @pl.when(n != t)
        def _():
            pl.semaphore_signal(barrier, inc=1, device_id=(x, n), device_id_type=MESH)

    @pl.loop(1, NX)
    def _(step):
        @pl.loop(0, 2 * NZ)
        def _(n):
            pl.semaphore_signal(barrier, inc=1, device_id=((x + step) % NX, y * 2 * NZ + n), device_id_type=MESH)

    @pl.when(x != y)
    def _():
        pl.semaphore_signal(barrier, inc=1, device_id=(y, partner), device_id_type=MESH)

    greeted = NY * 2 * NZ - 1 + (NX - 1) * 2 * NZ

    @pl.when(x != y)
    def _():
        pl.semaphore_wait(barrier, greeted + 1)

    @pl.when(x == y)
    def _():
        pl.semaphore_wait(barrier, greeted)

    home = G.at[x, 0, :, mine]

    @pl.when(x != y)
    def _():
        send(go, home, t_send, t_recv, y, x * 2 * NZ + z * 2 + c)

    @pl.when(x == y)
    def _():
        pltpu.make_async_copy(go, home, t_recv).start()

    east, west = (x + 1) % NX, (x + NX - 1) % NX
    pltpu.make_async_copy(acts, A.at[x], a_recv.at[0]).start()

    def start_acts():
        send(acts, A.at[x], a_send, a_recv.at[1], east, t)
        send(acts, A.at[x], a_send, a_recv.at[2], west, t)

    def pass_acts():
        wait(A.at[west], a_recv.at[1])
        piece = A.at[west, pl.ds(0, half)]
        send(piece, piece, a_send, a_recv.at[3], east, t)
        wait(A.at[east], a_recv.at[2])
        piece = A.at[east, pl.ds(half, half)]
        send(piece, piece, a_send, a_recv.at[3], west, t)

    def finish_acts():
        wait(A.at[x], a_recv.at[0])
        wait(A.at[(x + 2) % NX], a_recv.at[3])
        for d in range(NX):
            At[d] = A[d].T

    quarter = BLK // NX
    wide = V.shape[2]
    strip = weight.at[pl.ds(pl.multiple_of(x * quarter, quarter), quarter)]

    def start_weights():
        for step in range(NY):
            there = (y + step) % NY
            src = strip.at[:, pl.ds(pl.multiple_of(there * wide, wide), wide)]
            if step == 0:
                pltpu.make_async_copy(src, V.at[y], v_recv).start()
            else:
                send(src, V.at[y], v_send, v_recv, x, there * 2 * NZ + 2 * z + c)

    def pass_weights():
        wait(V, v_recv)
        dst = K.at[pl.ds(pl.multiple_of(BLK * (2 * z + c) + quarter * x, quarter), quarter)]

        @pl.loop(0, NX * 2 * NZ)
        def _(m):
            e, n = m // (2 * NZ), m % (2 * NZ)
            src = V.at[e, :, pl.ds(pl.multiple_of(n * 2 * BLK, 2 * BLK), 2 * BLK)]
            same = (e == x) & (n == 2 * z + c)

            @pl.when(same)
            def _():
                pltpu.make_async_copy(src, dst, w_recv).start()

            @pl.when(jnp.logical_not(same))
            def _():
                send(src, dst, w_send, w_recv, e, y * 2 * NZ + n)

    def finish_weights():
        wait(K, w_recv)

        @pl.loop(0, 2 * NZ)
        def _(f):
            rows = pl.ds(pl.multiple_of(f * BLK, BLK), BLK)
            for h in range(2):
                cols = slice(h * BLK, (h + 1) * BLK)
                K[rows, cols] = (K[rows, cols].astype(F32) * scalar(f, h)).astype(BF)

    def chunk(k):
        return (z + NZ + ((k + 1) // 2) * (1 - 2 * (k % 2))) % NZ

    def stage_z(k):
        block = G.at[y, k, :, mine]

        @pl.when(k == 0)
        def _():
            wait(block, t_recv)

        @pl.when(k > 0)
        def _():
            wait(block, z_recv.at[k])

        @pl.when((k == 0) | ((k % 2 == 1) & (k < 7)))
        def _():
            to_k = jnp.where(k == 0, 1, k + 2)
            send(block, G.at[y, to_k, :, mine], z_send, z_recv.at[to_k], x, right)

        @pl.when((k % 2 == 0) & (k < 6))
        def _():
            send(block, G.at[y, k + 2, :, mine], z_send, z_recv.at[k + 2], x, left)

        @pl.when(k < LEAD)
        def _():
            send(block, block, y_send, yp_recv.at[k], x, up)
            send(block, block, y_send, ym_recv.at[k], x, down)

        send(block, block, b_send, b_recv.at[0, k], x, mate)

    below, above, beyond = (y + NY - 1) % NY, (y + 1) % NY, (y + 2) % NY

    def stage_y(k):
        block = G.at[below, k, :, mine]
        wait(block, yp_recv.at[k])
        piece = G.at[below, k, low, mine]
        send(piece, piece, y_send, y2_recv.at[k], x, up)
        send(block, block, b_send, b_recv.at[1, k], x, mate)
        block = G.at[above, k, :, mine]
        wait(block, ym_recv.at[k])
        piece = G.at[above, k, high, mine]
        send(piece, piece, y_send, y2_recv.at[k], x, down)
        send(block, block, b_send, b_recv.at[2, k], x, mate)

    def stage_far(k):
        block = G.at[beyond, k, :, mine]
        wait(block, y2_recv.at[k])
        send(block, block, b_send, b_recv.at[3, k], x, mate)

    late = pl.ds(LEAD, NZ - LEAD)
    size = tokens // SLICES

    def rows_of(j, part_of=None):
        if part_of is None:
            return pl.ds(pl.multiple_of(j * size, size), size)
        return pl.ds(pl.multiple_of(j * size + part_of * (size // 2), size // 2), size // 2)

    def slice_start(j):
        block = G.at[y, late, rows_of(j), mine]
        send(block, block, y_send, yq_recv.at[j], x, up)
        send(block, block, y_send, yn_recv.at[j], x, down)

    def slice_y(j):
        block = G.at[below, late, rows_of(j), mine]
        wait(block, yq_recv.at[j])
        piece = G.at[below, late, rows_of(j, 0), mine]
        send(piece, piece, y_send, y3_recv.at[j], x, up)
        send(block, block, b_send, b2_recv.at[0, j], x, mate)
        block = G.at[above, late, rows_of(j), mine]
        wait(block, yn_recv.at[j])
        piece = G.at[above, late, rows_of(j, 1), mine]
        send(piece, piece, y_send, y3_recv.at[j], x, down)
        send(block, block, b_send, b2_recv.at[1, j], x, mate)

    def slice_far(j):
        block = G.at[beyond, late, rows_of(j), mine]
        wait(block, y3_recv.at[j])
        send(block, block, b_send, b2_recv.at[2, j], x, mate)

    def slice_input_grad(j):
        for kind, d in enumerate((below, above, beyond)):
            wait(G.at[d, late, rows_of(j), other], b2_recv.at[kind, j])

        @pl.loop(0, NX)
        def _(rel):
            d = (x + 2 + rel) % NX
            rows = rows_of(j)
            total = jnp.zeros((size, 2 * BLK), F32)
            for k in range(NZ):
                kept = K[pl.ds(pl.multiple_of(2 * BLK * chunk(k), 2 * BLK), 2 * BLK)]
                total += jnp.dot(G[d, k, rows], kept, preferred_element_type=F32)
            part[d, rows] = total

            @pl.when(rel == 0)
            def _():
                send(part.at[d, rows_of(j, 0)], H.at[0, j], r_send, h_recv.at[0, j], east, t)
                send(part.at[d, rows_of(j, 1)], H.at[1, j], r_send, h_recv.at[1, j], west, t)

            @pl.when(rel == 1)
            def _():
                send(part.at[d, rows_of(j, 0)], R.at[1, rows_of(j, 0)], r_send, r_recv.at[j], west, t)

            @pl.when(rel == 2)
            def _():
                pltpu.make_async_copy(part.at[d, rows_of(j)], own.at[rows_of(j)], o_recv).start()

            @pl.when(rel == 3)
            def _():
                send(part.at[d, rows_of(j, 1)], R.at[0, rows_of(j, 1)], r_send, r_recv.at[j], east, t)

    def slice_pass(j):
        wait(H.at[0, j], h_recv.at[0, j])
        part[east, rows_of(j, 0)] += H[0, j]
        send(part.at[east, rows_of(j, 0)], R.at[0, rows_of(j, 0)], r_send, r_recv.at[j], east, t)
        wait(H.at[1, j], h_recv.at[1, j])
        part[west, rows_of(j, 1)] += H[1, j]
        send(part.at[west, rows_of(j, 1)], R.at[1, rows_of(j, 1)], r_send, r_recv.at[j], west, t)

    def slice_finish(j):
        wait(R.at[:, rows_of(j)], r_recv.at[j])

    scale_factor = 1.0 / (tokens * NX) ** 0.5

    def stage_weight_grad(k):
        zc = chunk(k)

        @pl.when(k < LEAD)
        def _():
            for kind, d in enumerate((y, below, above, beyond)):
                wait(G.at[d, k, :, other], b_recv.at[kind, k])

        total = jnp.dot(At[0], G[0, k], preferred_element_type=F32)
        for d in range(1, NX):
            total += jnp.dot(At[d], G[d, k], preferred_element_type=F32)
        total = total.T * scale_factor
        for r in range(2):
            for h in range(2):
                tile = total[r * BLK:(r + 1) * BLK, h * BLK:(h + 1) * BLK] * scalar(2 * zc + r, h)
                tile = tile.reshape(4, BLK // 4, BLK)
                top = jnp.max(jnp.abs(tile), axis=1, keepdims=True)
                steps = (tile * jnp.where(top > 0, 1.0 / top, 0.0)) * STEPS
                here = (pl.ds(8 * zc + 4 * r, 4), slice(None), slice(h * BLK, (h + 1) * BLK))
                S[here] = jnp.round(steps).astype(jnp.int16)
                M[here] = top

        @pl.loop(0, 8)
        def _(j):
            n = 8 * zc + j

            @pl.when(n == t)
            def _():
                pltpu.make_async_copy(S.at[n], gw.at[:, columns], s_recv).start()
                pltpu.make_async_copy(M.at[n], gm.at[:, columns], m_recv).start()

            @pl.when(n != t)
            def _():
                send(S.at[n], gw.at[:, columns], s_send, s_recv, x, n)
                send(M.at[n], gm.at[:, columns], m_send, m_recv, x, n)

    @pl.loop(0, LEAD + 4)
    def _(i):
        @pl.when(i < NZ)
        def _():
            stage_z(i)

        @pl.when((i >= 2) & (i < LEAD + 2))
        def _():
            stage_y(i - 2)

        @pl.when(i == LEAD + 2)
        def _():
            pl.loop(0, SLICES)(slice_start)

        @pl.when((i >= 3) & (i < LEAD + 3))
        def _():
            stage_far(i - 3)

        @pl.when(i == 0)
        def _():
            start_acts()

        @pl.when(i == VSTART)
        def _():
            start_weights()

        @pl.when(i == 3)
        def _():
            pass_acts()

        @pl.when(i == VPASS)
        def _():
            pass_weights()

        @pl.when(i == 4)
        def _():
            finish_acts()

        @pl.when(i >= 4)
        def _():
            stage_weight_grad(i - 4)

    finish_weights()

    @pl.loop(LEAD, NZ)
    def _(k):
        wait(G.at[y, k, :, other], b_recv.at[0, k])

    @pl.loop(0, SLICES + 2)
    def _(i):
        @pl.when(i < SLICES)
        def _():
            slice_y(i)

        @pl.when((i >= 1) & (i < SLICES + 1))
        def _():
            slice_far(i - 1)

        @pl.when((i >= 2) & (i < SLICES + 2))
        def _():
            slice_input_grad(i - 2)

        @pl.when((i >= 3) & (i < SLICES + 2))
        def _():
            slice_pass(i - 3)

        @pl.when(i == SLICES + 1)
        def _():
            pl.loop(LEAD, NZ)(stage_weight_grad)

    slice_pass(SLICES - 1)
    pl.loop(0, SLICES)(slice_finish)
    wait(gw, s_recv)
    wait(gm, m_recv)
    wait(own, o_recv)

    @pl.when(x != y)
    def _():
        wait(go, t_send)

    wait(V.at[pl.ds(0, 3)], v_send)
    wait(K.at[pl.ds(0, 63 * quarter)], w_send)

    wait(A.at[pl.ds(0, 3)], a_send)
    wait(G.at[0, pl.ds(0, 7), :, pl.ds(0, BLK)], z_send)
    wait(G.at[pl.ds(0, 3), pl.ds(0, 4)], y_send)
    wait(G.at[pl.ds(0, 2)], b_send)
    wait(S.at[pl.ds(0, 63)], s_send)
    wait(M.at[pl.ds(0, 63)], m_send)
    wait(part.at[pl.ds(0, 3)], r_send)


def body(grad_out, acts, weight, block_mask):
    tokens, d_tile = grad_out.shape
    ff_tile = acts.shape[1]
    full_width = weight.shape[1]
    dma = pltpu.SemaphoreType.DMA
    own, sums, steps, top = pl.pallas_call(
        kernel,
        out_shape=(
            jax.ShapeDtypeStruct((tokens, ff_tile), F32),
            jax.ShapeDtypeStruct((2, tokens, ff_tile), F32),
            jax.ShapeDtypeStruct((d_tile // NX, full_width), jnp.int16),
            jax.ShapeDtypeStruct((1, full_width), F32),
        ),
        in_specs=[pl.BlockSpec(memory_space=pltpu.HBM)] * 3 + [pl.BlockSpec(memory_space=pltpu.SMEM)],
        out_specs=[pl.BlockSpec(memory_space=pltpu.HBM)] * 4,
        scratch_shapes=[
            pltpu.VMEM((NX, NZ, tokens, 2 * BLK), BF),
            pltpu.VMEM((NX, tokens, ff_tile), BF),
            pltpu.VMEM((NX, ff_tile, tokens), BF),
            pltpu.VMEM((NY, d_tile // NX, full_width // NY), BF),
            pltpu.VMEM((2 * NZ * BLK, ff_tile), BF),
            pltpu.VMEM((NX, tokens, ff_tile), F32),
            pltpu.VMEM((2, SLICES, tokens // SLICES // 2, ff_tile), F32),
            pltpu.VMEM((8 * NZ, BLK // NX, ff_tile), jnp.int16),
            pltpu.VMEM((8 * NZ, 1, ff_tile), F32),
        ] + [dma] * 10 + [dma, dma((4,)), dma, dma] + [dma((NZ,))] + [dma((LEAD,))] * 3 + [dma((SLICES,))] * 3
        + [dma((4, NZ)), dma((3, SLICES)), dma, dma, dma((2, SLICES)), dma((SLICES,)), dma],
        compiler_params=pltpu.CompilerParams(
            collective_id=0, has_side_effects=True, vmem_limit_bytes=63 * 1024 * 1024
        ),
    )(grad_out, acts, weight, block_mask)
    grad_acts = (own + sums[0] + sums[1]).astype(BF)
    grad_weight = (steps.astype(F32) * (1.0 / STEPS)) * top
    return grad_acts, grad_weight


def solution(mesh):
    in_specs = (P("dp", "tensor"), P("dp", "tensor"), P("tensor", None), P())
    out_specs = (P("dp", "tensor"), P(("dp", "tensor"), None))
    return jax.shard_map(body, mesh=mesh, in_specs=in_specs, out_specs=out_specs, check_vma=False)
```

```python
import jax
import jax.numpy as jnp
from jax import lax
from jax.experimental import pallas as pl
from jax.experimental.pallas import tpu as pltpu
from jax.sharding import PartitionSpec as P

NX, NY, NZ = 4, 4, 8
VSTART, VPASS = 0, 5
LEAD, SLICES = 6, 4
BLK = 128
BF, F32 = jnp.bfloat16, jnp.float32
STEPS = 32767.0
MESH = pl.DeviceIdType.MESH


def kernel(go, acts, weight, mask, own, R, gw, gm, G, A, At, V, K, part, H, S, M,
           t_send, a_send, v_send, w_send, z_send, y_send, b_send, s_send, m_send, r_send,
           t_recv, a_recv, v_recv, w_recv, z_recv, yp_recv, ym_recv, y2_recv,
           yq_recv, yn_recv, y3_recv, b_recv, b2_recv, s_recv, m_recv, h_recv, r_recv, o_recv):
    x = lax.axis_index("dp")
    t = lax.axis_index("tensor")
    y, z, c = t // (2 * NZ), (t % (2 * NZ)) // 2, t % 2
    mine = pl.ds(pl.multiple_of(c * BLK, BLK), BLK)
    other = pl.ds(pl.multiple_of((1 - c) * BLK, BLK), BLK)
    columns = pl.ds(pl.multiple_of(t * 2 * BLK, 2 * BLK), 2 * BLK)
    tokens = go.shape[0]
    half = tokens // 2
    low, high = pl.ds(0, half), pl.ds(half, half)
    mate = y * 2 * NZ + z * 2 + (1 - c)
    up = ((y + 1) % NY) * 2 * NZ + z * 2 + c
    down = ((y + NY - 1) % NY) * 2 * NZ + z * 2 + c
    right = y * 2 * NZ + ((z + 1) % NZ) * 2 + c
    left = y * 2 * NZ + ((z + NZ - 1) % NZ) * 2 + c

    def send(src, dst, send_sem, recv_sem, to_x, to_t):
        pltpu.make_async_remote_copy(
            src_ref=src, dst_ref=dst, send_sem=send_sem, recv_sem=recv_sem,
            device_id=(to_x, to_t), device_id_type=MESH,
        ).start()

    def wait(region, sem):
        pltpu.make_async_copy(region, region, sem).wait()

    def scalar(row, h):
        return mask[x * 2 * NZ + row, 2 * t + h].astype(F32)

    barrier = pltpu.get_barrier_semaphore()
    partner = x * 2 * NZ + z * 2 + c

    @pl.loop(0, NY * 2 * NZ)
    def _(n):
        @pl.when(n != t)
        def _():
            pl.semaphore_signal(barrier, inc=1, device_id=(x, n), device_id_type=MESH)

    @pl.loop(1, NX)
    def _(step):
        @pl.loop(0, 2 * NZ)
        def _(n):
            pl.semaphore_signal(barrier, inc=1, device_id=((x + step) % NX, y * 2 * NZ + n), device_id_type=MESH)

    @pl.when(x != y)
    def _():
        pl.semaphore_signal(barrier, inc=1, device_id=(y, partner), device_id_type=MESH)

    greeted = NY * 2 * NZ - 1 + (NX - 1) * 2 * NZ

    @pl.when(x != y)
    def _():
        pl.semaphore_wait(barrier, greeted + 1)

    @pl.when(x == y)
    def _():
        pl.semaphore_wait(barrier, greeted)


    for part_of, rows in enumerate((low, high)):
        @pl.when(x != y)
        def _():
            send(go.at[rows], G.at[x, 0, rows, mine], t_send, t_recv.at[part_of], y, partner)

        @pl.when(x == y)
        def _():
            pltpu.make_async_copy(go.at[rows], G.at[x, 0, rows, mine], t_recv.at[part_of]).start()

    east, west = (x + 1) % NX, (x + NX - 1) % NX
    pltpu.make_async_copy(acts, A.at[x], a_recv.at[0]).start()

    def start_acts():
        send(acts, A.at[x], a_send, a_recv.at[1], east, t)
        send(acts, A.at[x], a_send, a_recv.at[2], west, t)

    def pass_acts():
        wait(A.at[west], a_recv.at[1])
        piece = A.at[west, pl.ds(0, half)]
        send(piece, piece, a_send, a_recv.at[3], east, t)
        wait(A.at[east], a_recv.at[2])
        piece = A.at[east, pl.ds(half, half)]
        send(piece, piece, a_send, a_recv.at[3], west, t)

    def finish_acts():
        wait(A.at[x], a_recv.at[0])
        wait(A.at[(x + 2) % NX], a_recv.at[3])
        for d in range(NX):
            At[d] = A[d].T

    quarter = BLK // NX
    wide = V.shape[2]
    strip = weight.at[pl.ds(pl.multiple_of(x * quarter, quarter), quarter)]

    def start_weights():
        for step in range(NY):
            there = (y + step) % NY
            src = strip.at[:, pl.ds(pl.multiple_of(there * wide, wide), wide)]
            if step == 0:
                pltpu.make_async_copy(src, V.at[y], v_recv).start()
            else:
                send(src, V.at[y], v_send, v_recv, x, there * 2 * NZ + 2 * z + c)

    def pass_weights():
        wait(V, v_recv)
        dst = K.at[pl.ds(pl.multiple_of(BLK * (2 * z + c) + quarter * x, quarter), quarter)]

        @pl.loop(0, NX * 2 * NZ)
        def _(m):
            e, n = m // (2 * NZ), m % (2 * NZ)
            src = V.at[e, :, pl.ds(pl.multiple_of(n * 2 * BLK, 2 * BLK), 2 * BLK)]
            same = (e == x) & (n == 2 * z + c)

            @pl.when(same)
            def _():
                pltpu.make_async_copy(src, dst, w_recv).start()

            @pl.when(jnp.logical_not(same))
            def _():
                send(src, dst, w_send, w_recv, e, y * 2 * NZ + n)

    def finish_weights():
        wait(K, w_recv)

        @pl.loop(0, 2 * NZ)
        def _(f):
            rows = pl.ds(pl.multiple_of(f * BLK, BLK), BLK)
            for h in range(2):
                cols = slice(h * BLK, (h + 1) * BLK)
                K[rows, cols] = (K[rows, cols].astype(F32) * scalar(f, h)).astype(BF)

    def chunk(k):
        return (z + NZ + ((k + 1) // 2) * (1 - 2 * (k % 2))) % NZ

    def stage_z(k):
        block = G.at[y, k, :, mine]

        @pl.when(k == 0)
        def _():
            for part_of, rows in enumerate((low, high)):
                piece = G.at[y, k, rows, mine]
                wait(piece, t_recv.at[part_of])
                send(piece, piece, y_send, yp_recv.at[k], x, up)
                send(piece, piece, y_send, ym_recv.at[k], x, down)

        @pl.when(k > 0)
        def _():
            wait(block, z_recv.at[k])

        @pl.when((k == 0) | ((k % 2 == 1) & (k < 7)))
        def _():
            to_k = jnp.where(k == 0, 1, k + 2)
            send(block, G.at[y, to_k, :, mine], z_send, z_recv.at[to_k], x, right)

        @pl.when((k % 2 == 0) & (k < 6))
        def _():
            send(block, G.at[y, k + 2, :, mine], z_send, z_recv.at[k + 2], x, left)

        @pl.when((k > 0) & (k < LEAD))
        def _():
            send(block, block, y_send, yp_recv.at[k], x, up)
            send(block, block, y_send, ym_recv.at[k], x, down)

        send(block, block, b_send, b_recv.at[0, k], x, mate)

    below, above, beyond = (y + NY - 1) % NY, (y + 1) % NY, (y + 2) % NY

    def stage_y(k):
        block = G.at[below, k, :, mine]
        wait(block, yp_recv.at[k])
        piece = G.at[below, k, low, mine]
        send(piece, piece, y_send, y2_recv.at[k], x, up)
        send(block, block, b_send, b_recv.at[1, k], x, mate)
        block = G.at[above, k, :, mine]
        wait(block, ym_recv.at[k])
        piece = G.at[above, k, high, mine]
        send(piece, piece, y_send, y2_recv.at[k], x, down)
        send(block, block, b_send, b_recv.at[2, k], x, mate)

    def stage_far(k):
        block = G.at[beyond, k, :, mine]
        wait(block, y2_recv.at[k])
        send(block, block, b_send, b_recv.at[3, k], x, mate)

    late = pl.ds(LEAD, NZ - LEAD)
    size = tokens // SLICES

    def rows_of(j, part_of=None):
        if part_of is None:
            return pl.ds(pl.multiple_of(j * size, size), size)
        return pl.ds(pl.multiple_of(j * size + part_of * (size // 2), size // 2), size // 2)

    def slice_start(j):
        block = G.at[y, late, rows_of(j), mine]
        send(block, block, y_send, yq_recv.at[j], x, up)
        send(block, block, y_send, yn_recv.at[j], x, down)

    def slice_y(j):
        block = G.at[below, late, rows_of(j), mine]
        wait(block, yq_recv.at[j])
        piece = G.at[below, late, rows_of(j, 0), mine]
        send(piece, piece, y_send, y3_recv.at[j], x, up)
        send(block, block, b_send, b2_recv.at[0, j], x, mate)
        block = G.at[above, late, rows_of(j), mine]
        wait(block, yn_recv.at[j])
        piece = G.at[above, late, rows_of(j, 1), mine]
        send(piece, piece, y_send, y3_recv.at[j], x, down)
        send(block, block, b_send, b2_recv.at[1, j], x, mate)

    def slice_far(j):
        block = G.at[beyond, late, rows_of(j), mine]
        wait(block, y3_recv.at[j])
        send(block, block, b_send, b2_recv.at[2, j], x, mate)

    def slice_input_grad(j):
        for kind, d in enumerate((below, above, beyond)):
            wait(G.at[d, late, rows_of(j), other], b2_recv.at[kind, j])

        @pl.loop(0, NX)
        def _(rel):
            d = (x + 2 + rel) % NX
            rows = rows_of(j)
            total = jnp.zeros((size, 2 * BLK), F32)
            for k in range(NZ):
                kept = K[pl.ds(pl.multiple_of(2 * BLK * chunk(k), 2 * BLK), 2 * BLK)]
                total += jnp.dot(G[d, k, rows], kept, preferred_element_type=F32)
            part[d, rows] = total

            @pl.when(rel == 0)
            def _():
                send(part.at[d, rows_of(j, 0)], H.at[0, j], r_send, h_recv.at[0, j], east, t)
                send(part.at[d, rows_of(j, 1)], H.at[1, j], r_send, h_recv.at[1, j], west, t)

            @pl.when(rel == 1)
            def _():
                send(part.at[d, rows_of(j, 0)], R.at[1, rows_of(j, 0)], r_send, r_recv.at[j], west, t)

            @pl.when(rel == 2)
            def _():
                pltpu.make_async_copy(part.at[d, rows_of(j)], own.at[rows_of(j)], o_recv).start()

            @pl.when(rel == 3)
            def _():
                send(part.at[d, rows_of(j, 1)], R.at[0, rows_of(j, 1)], r_send, r_recv.at[j], east, t)

    def slice_pass(j):
        wait(H.at[0, j], h_recv.at[0, j])
        part[east, rows_of(j, 0)] += H[0, j]
        send(part.at[east, rows_of(j, 0)], R.at[0, rows_of(j, 0)], r_send, r_recv.at[j], east, t)
        wait(H.at[1, j], h_recv.at[1, j])
        part[west, rows_of(j, 1)] += H[1, j]
        send(part.at[west, rows_of(j, 1)], R.at[1, rows_of(j, 1)], r_send, r_recv.at[j], west, t)

    def slice_finish(j):
        wait(R.at[:, rows_of(j)], r_recv.at[j])

    scale_factor = 1.0 / (tokens * NX) ** 0.5

    def stage_weight_grad(k):
        zc = chunk(k)

        @pl.when(k < LEAD)
        def _():
            for kind, d in enumerate((y, below, above, beyond)):
                wait(G.at[d, k, :, other], b_recv.at[kind, k])

        total = jnp.dot(At[0], G[0, k], preferred_element_type=F32)
        for d in range(1, NX):
            total += jnp.dot(At[d], G[d, k], preferred_element_type=F32)
        total = total.T * scale_factor
        for r in range(2):
            for h in range(2):
                tile = total[r * BLK:(r + 1) * BLK, h * BLK:(h + 1) * BLK] * scalar(2 * zc + r, h)
                tile = tile.reshape(4, BLK // 4, BLK)
                top = jnp.max(jnp.abs(tile), axis=1, keepdims=True)
                steps = (tile * jnp.where(top > 0, 1.0 / top, 0.0)) * STEPS
                here = (pl.ds(8 * zc + 4 * r, 4), slice(None), slice(h * BLK, (h + 1) * BLK))
                S[here] = jnp.round(steps).astype(jnp.int16)
                M[here] = top

        @pl.loop(0, 8)
        def _(j):
            n = 8 * zc + j

            @pl.when(n == t)
            def _():
                pltpu.make_async_copy(S.at[n], gw.at[:, columns], s_recv).start()
                pltpu.make_async_copy(M.at[n], gm.at[:, columns], m_recv).start()

            @pl.when(n != t)
            def _():
                send(S.at[n], gw.at[:, columns], s_send, s_recv, x, n)
                send(M.at[n], gm.at[:, columns], m_send, m_recv, x, n)

    @pl.loop(0, LEAD + 4)
    def _(i):
        @pl.when(i < NZ)
        def _():
            stage_z(i)

        @pl.when((i >= 2) & (i < LEAD + 2))
        def _():
            stage_y(i - 2)

        @pl.when(i == LEAD + 2)
        def _():
            pl.loop(0, SLICES)(slice_start)

        @pl.when((i >= 3) & (i < LEAD + 3))
        def _():
            stage_far(i - 3)

        @pl.when(i == 0)
        def _():
            start_acts()

        @pl.when(i == VSTART)
        def _():
            start_weights()

        @pl.when(i == 3)
        def _():
            pass_acts()

        @pl.when(i == VPASS)
        def _():
            pass_weights()

        @pl.when(i == 4)
        def _():
            finish_acts()

        @pl.when(i >= 4)
        def _():
            stage_weight_grad(i - 4)

    @pl.loop(0, SLICES + 2)
    def _(i):
        @pl.when(i < SLICES)
        def _():
            slice_y(i)

        @pl.when((i >= 1) & (i < SLICES + 1))
        def _():
            slice_far(i - 1)

        @pl.when(i == 2)
        def _():
            finish_weights()

            @pl.loop(LEAD, NZ)
            def _(k):
                wait(G.at[y, k, :, other], b_recv.at[0, k])

        @pl.when((i >= 2) & (i < SLICES + 2))
        def _():
            slice_input_grad(i - 2)

        @pl.when((i >= 3) & (i < SLICES + 2))
        def _():
            slice_pass(i - 3)

        @pl.when(i == SLICES + 1)
        def _():
            pl.loop(LEAD, NZ)(stage_weight_grad)

    slice_pass(SLICES - 1)
    pl.loop(0, SLICES)(slice_finish)
    wait(gw, s_recv)
    wait(gm, m_recv)
    wait(own, o_recv)

    @pl.when(x != y)
    def _():
        wait(go, t_send)

    wait(V.at[pl.ds(0, 3)], v_send)
    wait(K.at[pl.ds(0, 63 * quarter)], w_send)

    wait(A.at[pl.ds(0, 3)], a_send)
    wait(G.at[0, pl.ds(0, 7), :, pl.ds(0, BLK)], z_send)
    wait(G.at[pl.ds(0, 3), pl.ds(0, 4)], y_send)
    wait(G.at[pl.ds(0, 2)], b_send)
    wait(S.at[pl.ds(0, 63)], s_send)
    wait(M.at[pl.ds(0, 63)], m_send)
    wait(part.at[pl.ds(0, 3)], r_send)


def body(grad_out, acts, weight, block_mask):
    tokens, d_tile = grad_out.shape
    ff_tile = acts.shape[1]
    full_width = weight.shape[1]
    dma = pltpu.SemaphoreType.DMA
    own, sums, steps, top = pl.pallas_call(
        kernel,
        out_shape=(
            jax.ShapeDtypeStruct((tokens, ff_tile), F32),
            jax.ShapeDtypeStruct((2, tokens, ff_tile), F32),
            jax.ShapeDtypeStruct((d_tile // NX, full_width), jnp.int16),
            jax.ShapeDtypeStruct((1, full_width), F32),
        ),
        in_specs=[pl.BlockSpec(memory_space=pltpu.HBM)] * 3 + [pl.BlockSpec(memory_space=pltpu.SMEM)],
        out_specs=[pl.BlockSpec(memory_space=pltpu.HBM)] * 4,
        scratch_shapes=[
            pltpu.VMEM((NX, NZ, tokens, 2 * BLK), BF),
            pltpu.VMEM((NX, tokens, ff_tile), BF),
            pltpu.VMEM((NX, ff_tile, tokens), BF),
            pltpu.VMEM((NY, d_tile // NX, full_width // NY), BF),
            pltpu.VMEM((2 * NZ * BLK, ff_tile), BF),
            pltpu.VMEM((NX, tokens, ff_tile), F32),
            pltpu.VMEM((2, SLICES, tokens // SLICES // 2, ff_tile), F32),
            pltpu.VMEM((8 * NZ, BLK // NX, ff_tile), jnp.int16),
            pltpu.VMEM((8 * NZ, 1, ff_tile), F32),
        ] + [dma] * 10 + [dma((2,)), dma((4,)), dma, dma] + [dma((NZ,))] + [dma((LEAD,))] * 3 + [dma((SLICES,))] * 3
        + [dma((4, NZ)), dma((3, SLICES)), dma, dma, dma((2, SLICES)), dma((SLICES,)), dma],
        compiler_params=pltpu.CompilerParams(
            collective_id=0, has_side_effects=True, vmem_limit_bytes=63 * 1024 * 1024
        ),
    )(grad_out, acts, weight, block_mask)
    grad_acts = (own + sums[0] + sums[1]).astype(BF)
    grad_weight = (steps.astype(F32) * (1.0 / STEPS)) * top
    return grad_acts, grad_weight


def solution(mesh):
    in_specs = (P("dp", "tensor"), P("dp", "tensor"), P("tensor", None), P())
    out_specs = (P("dp", "tensor"), P(("dp", "tensor"), None))
    return jax.shard_map(body, mesh=mesh, in_specs=in_specs, out_specs=out_specs, check_vma=False)
```

```python
import jax
import jax.numpy as jnp
from jax import lax
from jax.experimental import pallas as pl
from jax.experimental.pallas import tpu as pltpu
from jax.sharding import PartitionSpec as P

NX, NY, NZ = 4, 4, 8
VPASS = 5
LEAD, SLICES = 5, 4
BLK = 128
BF, F32 = jnp.bfloat16, jnp.float32
STEPS = 32767.0
MESH = pl.DeviceIdType.MESH


def kernel(go, acts, weight, mask, own, R, gw, gm, G, A, At, V, K, part, H, S, M,
           t_send, a_send, v_send, w_send, z_send, y_send, b_send, s_send, m_send, r_send,
           t_recv, a_recv, v_recv, w_recv, z_recv, yp_recv, ym_recv, y2_recv,
           yq_recv, yn_recv, y3_recv, b_recv, b2_recv, s_recv, m_recv, h_recv, r_recv, o_recv):
    x = lax.axis_index("dp")
    t = lax.axis_index("tensor")
    y, z, c = t // (2 * NZ), (t % (2 * NZ)) // 2, t % 2
    mine = pl.ds(pl.multiple_of(c * BLK, BLK), BLK)
    other = pl.ds(pl.multiple_of((1 - c) * BLK, BLK), BLK)
    columns = pl.ds(pl.multiple_of(t * 2 * BLK, 2 * BLK), 2 * BLK)
    tokens = go.shape[0]
    half = tokens // 2
    low, high = pl.ds(0, half), pl.ds(half, half)
    mate = y * 2 * NZ + z * 2 + (1 - c)
    up = ((y + 1) % NY) * 2 * NZ + z * 2 + c
    down = ((y + NY - 1) % NY) * 2 * NZ + z * 2 + c
    right = y * 2 * NZ + ((z + 1) % NZ) * 2 + c
    left = y * 2 * NZ + ((z + NZ - 1) % NZ) * 2 + c

    def send(src, dst, send_sem, recv_sem, to_x, to_t):
        pltpu.make_async_remote_copy(
            src_ref=src, dst_ref=dst, send_sem=send_sem, recv_sem=recv_sem,
            device_id=(to_x, to_t), device_id_type=MESH,
        ).start()

    def wait(region, sem):
        pltpu.make_async_copy(region, region, sem).wait()

    def scalar(row, h):
        return mask[x * 2 * NZ + row, 2 * t + h].astype(F32)

    barrier = pltpu.get_barrier_semaphore()
    partner = x * 2 * NZ + z * 2 + c

    @pl.loop(0, NY * 2 * NZ)
    def _(n):
        @pl.when(n != t)
        def _():
            pl.semaphore_signal(barrier, inc=1, device_id=(x, n), device_id_type=MESH)

    @pl.loop(1, NX)
    def _(step):
        @pl.loop(0, 2 * NZ)
        def _(n):
            pl.semaphore_signal(barrier, inc=1, device_id=((x + step) % NX, y * 2 * NZ + n), device_id_type=MESH)

    @pl.when(x != y)
    def _():
        pl.semaphore_signal(barrier, inc=1, device_id=(y, partner), device_id_type=MESH)

    greeted = NY * 2 * NZ - 1 + (NX - 1) * 2 * NZ

    @pl.when(x != y)
    def _():
        pl.semaphore_wait(barrier, greeted + 1)

    @pl.when(x == y)
    def _():
        pl.semaphore_wait(barrier, greeted)


    for part_of, rows in enumerate((low, high)):
        @pl.when(x != y)
        def _():
            send(go.at[rows], G.at[x, 0, rows, mine], t_send, t_recv.at[part_of], y, partner)

        @pl.when(x == y)
        def _():
            pltpu.make_async_copy(go.at[rows], G.at[x, 0, rows, mine], t_recv.at[part_of]).start()

    east, west = (x + 1) % NX, (x + NX - 1) % NX
    pltpu.make_async_copy(acts, A.at[x], a_recv.at[0]).start()

    def start_acts():
        send(acts, A.at[x], a_send, a_recv.at[1], east, t)
        send(acts, A.at[x], a_send, a_recv.at[2], west, t)

    def pass_acts():
        wait(A.at[west], a_recv.at[1])
        piece = A.at[west, pl.ds(0, half)]
        send(piece, piece, a_send, a_recv.at[3], east, t)
        wait(A.at[east], a_recv.at[2])
        piece = A.at[east, pl.ds(half, half)]
        send(piece, piece, a_send, a_recv.at[3], west, t)

    def finish_acts():
        wait(A.at[x], a_recv.at[0])
        wait(A.at[(x + 2) % NX], a_recv.at[3])
        for d in range(NX):
            At[d] = A[d].T

    quarter = BLK // NX
    wide = V.shape[2]
    strip = weight.at[pl.ds(pl.multiple_of(x * quarter, quarter), quarter)]

    def start_weights():
        for step in range(NY):
            there = (y + step) % NY
            src = strip.at[:, pl.ds(pl.multiple_of(there * wide, wide), wide)]
            if step == 0:
                pltpu.make_async_copy(src, V.at[y], v_recv).start()
            else:
                send(src, V.at[y], v_send, v_recv, x, there * 2 * NZ + 2 * z + c)

    def pass_weights():
        wait(V, v_recv)
        dst = K.at[pl.ds(pl.multiple_of(BLK * (2 * z + c) + quarter * x, quarter), quarter)]

        @pl.loop(0, NX * 2 * NZ)
        def _(m):
            e, n = m // (2 * NZ), m % (2 * NZ)
            src = V.at[e, :, pl.ds(pl.multiple_of(n * 2 * BLK, 2 * BLK), 2 * BLK)]
            same = (e == x) & (n == 2 * z + c)

            @pl.when(same)
            def _():
                pltpu.make_async_copy(src, dst, w_recv).start()

            @pl.when(jnp.logical_not(same))
            def _():
                send(src, dst, w_send, w_recv, e, y * 2 * NZ + n)

    def finish_weights():
        wait(K, w_recv)

        @pl.loop(0, 2 * NZ)
        def _(f):
            rows = pl.ds(pl.multiple_of(f * BLK, BLK), BLK)
            for h in range(2):
                cols = slice(h * BLK, (h + 1) * BLK)
                K[rows, cols] = (K[rows, cols].astype(F32) * scalar(f, h)).astype(BF)

    start_weights()

    def chunk(k):
        return (z + NZ + ((k + 1) // 2) * (1 - 2 * (k % 2))) % NZ

    def stage_z(k):
        block = G.at[y, k, :, mine]

        @pl.when(k == 0)
        def _():
            for part_of, rows in enumerate((low, high)):
                piece = G.at[y, k, rows, mine]
                wait(piece, t_recv.at[part_of])
                send(piece, piece, y_send, yp_recv.at[k], x, up)
                send(piece, piece, y_send, ym_recv.at[k], x, down)

        @pl.when(k > 0)
        def _():
            wait(block, z_recv.at[k])

        @pl.when((k == 0) | ((k % 2 == 1) & (k < 7)))
        def _():
            to_k = jnp.where(k == 0, 1, k + 2)
            send(block, G.at[y, to_k, :, mine], z_send, z_recv.at[to_k], x, right)

        @pl.when((k % 2 == 0) & (k < 6))
        def _():
            send(block, G.at[y, k + 2, :, mine], z_send, z_recv.at[k + 2], x, left)

        @pl.when((k > 0) & (k < LEAD))
        def _():
            send(block, block, y_send, yp_recv.at[k], x, up)
            send(block, block, y_send, ym_recv.at[k], x, down)

        send(block, block, b_send, b_recv.at[0, k], x, mate)

    below, above, beyond = (y + NY - 1) % NY, (y + 1) % NY, (y + 2) % NY

    def stage_y(k):
        block = G.at[below, k, :, mine]
        wait(block, yp_recv.at[k])
        piece = G.at[below, k, low, mine]
        send(piece, piece, y_send, y2_recv.at[k], x, up)
        send(block, block, b_send, b_recv.at[1, k], x, mate)
        block = G.at[above, k, :, mine]
        wait(block, ym_recv.at[k])
        piece = G.at[above, k, high, mine]
        send(piece, piece, y_send, y2_recv.at[k], x, down)
        send(block, block, b_send, b_recv.at[2, k], x, mate)

    def stage_far(k):
        block = G.at[beyond, k, :, mine]
        wait(block, y2_recv.at[k])
        send(block, block, b_send, b_recv.at[3, k], x, mate)

    late = pl.ds(LEAD, NZ - LEAD)
    size = tokens // SLICES

    def rows_of(j, part_of=None):
        if part_of is None:
            return pl.ds(pl.multiple_of(j * size, size), size)
        return pl.ds(pl.multiple_of(j * size + part_of * (size // 2), size // 2), size // 2)

    def slice_start(j):
        block = G.at[y, late, rows_of(j), mine]
        send(block, block, y_send, yq_recv.at[j], x, up)
        send(block, block, y_send, yn_recv.at[j], x, down)

    def slice_y(j):
        block = G.at[below, late, rows_of(j), mine]
        wait(block, yq_recv.at[j])
        piece = G.at[below, late, rows_of(j, 0), mine]
        send(piece, piece, y_send, y3_recv.at[j], x, up)
        send(block, block, b_send, b2_recv.at[0, j], x, mate)
        block = G.at[above, late, rows_of(j), mine]
        wait(block, yn_recv.at[j])
        piece = G.at[above, late, rows_of(j, 1), mine]
        send(piece, piece, y_send, y3_recv.at[j], x, down)
        send(block, block, b_send, b2_recv.at[1, j], x, mate)

    def slice_far(j):
        block = G.at[beyond, late, rows_of(j), mine]
        wait(block, y3_recv.at[j])
        send(block, block, b_send, b2_recv.at[2, j], x, mate)

    def slice_input_grad(j):
        for kind, d in enumerate((below, above, beyond)):
            wait(G.at[d, late, rows_of(j), other], b2_recv.at[kind, j])

        @pl.loop(0, NX)
        def _(rel):
            d = (x + 2 + rel) % NX
            rows = rows_of(j)
            total = jnp.zeros((size, 2 * BLK), F32)
            for k in range(NZ):
                kept = K[pl.ds(pl.multiple_of(2 * BLK * chunk(k), 2 * BLK), 2 * BLK)]
                total += jnp.dot(G[d, k, rows], kept, preferred_element_type=F32)
            part[d, rows] = total

            @pl.when(rel == 0)
            def _():
                send(part.at[d, rows_of(j, 0)], H.at[0, j], r_send, h_recv.at[0, j], east, t)
                send(part.at[d, rows_of(j, 1)], H.at[1, j], r_send, h_recv.at[1, j], west, t)

            @pl.when(rel == 1)
            def _():
                send(part.at[d, rows_of(j, 0)], R.at[1, rows_of(j, 0)], r_send, r_recv.at[j], west, t)

            @pl.when(rel == 2)
            def _():
                pltpu.make_async_copy(part.at[d, rows_of(j)], own.at[rows_of(j)], o_recv).start()

            @pl.when(rel == 3)
            def _():
                send(part.at[d, rows_of(j, 1)], R.at[0, rows_of(j, 1)], r_send, r_recv.at[j], east, t)

    def slice_pass(j):
        wait(H.at[0, j], h_recv.at[0, j])
        part[east, rows_of(j, 0)] += H[0, j]
        send(part.at[east, rows_of(j, 0)], R.at[0, rows_of(j, 0)], r_send, r_recv.at[j], east, t)
        wait(H.at[1, j], h_recv.at[1, j])
        part[west, rows_of(j, 1)] += H[1, j]
        send(part.at[west, rows_of(j, 1)], R.at[1, rows_of(j, 1)], r_send, r_recv.at[j], west, t)

    def slice_finish(j):
        wait(R.at[:, rows_of(j)], r_recv.at[j])

    scale_factor = 1.0 / (tokens * NX) ** 0.5

    def stage_weight_grad(k):
        zc = chunk(k)

        @pl.when(k < LEAD)
        def _():
            for kind, d in enumerate((y, below, above, beyond)):
                wait(G.at[d, k, :, other], b_recv.at[kind, k])

        total = jnp.dot(At[0], G[0, k], preferred_element_type=F32)
        for d in range(1, NX):
            total += jnp.dot(At[d], G[d, k], preferred_element_type=F32)
        total = total.T * scale_factor
        for r in range(2):
            for h in range(2):
                tile = total[r * BLK:(r + 1) * BLK, h * BLK:(h + 1) * BLK] * scalar(2 * zc + r, h)
                tile = tile.reshape(4, BLK // 4, BLK)
                top = jnp.max(jnp.abs(tile), axis=1, keepdims=True)
                steps = (tile * jnp.where(top > 0, 1.0 / top, 0.0)) * STEPS
                here = (pl.ds(8 * zc + 4 * r, 4), slice(None), slice(h * BLK, (h + 1) * BLK))
                S[here] = jnp.round(steps).astype(jnp.int16)
                M[here] = top

        @pl.loop(0, 8)
        def _(j):
            n = 8 * zc + j

            @pl.when(n == t)
            def _():
                pltpu.make_async_copy(S.at[n], gw.at[:, columns], s_recv).start()
                pltpu.make_async_copy(M.at[n], gm.at[:, columns], m_recv).start()

            @pl.when(n != t)
            def _():
                send(S.at[n], gw.at[:, columns], s_send, s_recv, x, n)
                send(M.at[n], gm.at[:, columns], m_send, m_recv, x, n)

    @pl.loop(0, LEAD + 4)
    def _(i):
        @pl.when(i < NZ)
        def _():
            stage_z(i)

        @pl.when((i >= 2) & (i < LEAD + 2))
        def _():
            stage_y(i - 2)

        @pl.when(i == LEAD + 2)
        def _():
            pl.loop(0, SLICES)(slice_start)

        @pl.when((i >= 3) & (i < LEAD + 3))
        def _():
            stage_far(i - 3)

        @pl.when(i == 0)
        def _():
            start_acts()

        @pl.when(i == 3)
        def _():
            pass_acts()

        @pl.when(i == VPASS)
        def _():
            pass_weights()

        @pl.when(i == 4)
        def _():
            finish_acts()

        @pl.when(i >= 4)
        def _():
            stage_weight_grad(i - 4)

    @pl.loop(0, SLICES + 2)
    def _(i):
        @pl.when(i < SLICES)
        def _():
            slice_y(i)

        @pl.when((i >= 1) & (i < SLICES + 1))
        def _():
            slice_far(i - 1)

        @pl.when(i == 2)
        def _():
            finish_weights()

            @pl.loop(LEAD, NZ)
            def _(k):
                wait(G.at[y, k, :, other], b_recv.at[0, k])

        @pl.when((i >= 2) & (i < SLICES + 2))
        def _():
            slice_input_grad(i - 2)

        @pl.when((i >= 3) & (i < SLICES + 2))
        def _():
            slice_pass(i - 3)

        @pl.when(i == SLICES + 1)
        def _():
            pl.loop(LEAD, NZ)(stage_weight_grad)

    slice_pass(SLICES - 1)
    pl.loop(0, SLICES)(slice_finish)
    wait(gw, s_recv)
    wait(gm, m_recv)
    wait(own, o_recv)

    @pl.when(x != y)
    def _():
        wait(go, t_send)

    wait(V.at[pl.ds(0, 3)], v_send)
    wait(K.at[pl.ds(0, 63 * quarter)], w_send)

    wait(A.at[pl.ds(0, 3)], a_send)
    wait(G.at[0, pl.ds(0, 7), :, pl.ds(0, BLK)], z_send)
    wait(G.at[pl.ds(0, 3), pl.ds(0, 4)], y_send)
    wait(G.at[pl.ds(0, 2)], b_send)
    wait(S.at[pl.ds(0, 63)], s_send)
    wait(M.at[pl.ds(0, 63)], m_send)
    wait(part.at[pl.ds(0, 3)], r_send)


def body(grad_out, acts, weight, block_mask):
    tokens, d_tile = grad_out.shape
    ff_tile = acts.shape[1]
    full_width = weight.shape[1]
    dma = pltpu.SemaphoreType.DMA
    own, sums, steps, top = pl.pallas_call(
        kernel,
        out_shape=(
            jax.ShapeDtypeStruct((tokens, ff_tile), F32),
            jax.ShapeDtypeStruct((2, tokens, ff_tile), F32),
            jax.ShapeDtypeStruct((d_tile // NX, full_width), jnp.int16),
            jax.ShapeDtypeStruct((1, full_width), F32),
        ),
        in_specs=[pl.BlockSpec(memory_space=pltpu.HBM)] * 3 + [pl.BlockSpec(memory_space=pltpu.SMEM)],
        out_specs=[pl.BlockSpec(memory_space=pltpu.HBM)] * 4,
        scratch_shapes=[
            pltpu.VMEM((NX, NZ, tokens, 2 * BLK), BF),
            pltpu.VMEM((NX, tokens, ff_tile), BF),
            pltpu.VMEM((NX, ff_tile, tokens), BF),
            pltpu.VMEM((NY, d_tile // NX, full_width // NY), BF),
            pltpu.VMEM((2 * NZ * BLK, ff_tile), BF),
            pltpu.VMEM((NX, tokens, ff_tile), F32),
            pltpu.VMEM((2, SLICES, tokens // SLICES // 2, ff_tile), F32),
            pltpu.VMEM((8 * NZ, BLK // NX, ff_tile), jnp.int16),
            pltpu.VMEM((8 * NZ, 1, ff_tile), F32),
        ] + [dma] * 10 + [dma((2,)), dma((4,)), dma, dma] + [dma((NZ,))] + [dma((LEAD,))] * 3 + [dma((SLICES,))] * 3
        + [dma((4, NZ)), dma((3, SLICES)), dma, dma, dma((2, SLICES)), dma((SLICES,)), dma],
        compiler_params=pltpu.CompilerParams(
            collective_id=0, has_side_effects=True, vmem_limit_bytes=63 * 1024 * 1024
        ),
    )(grad_out, acts, weight, block_mask)
    grad_acts = (own + sums[0] + sums[1]).astype(BF)
    grad_weight = (steps.astype(F32) * (1.0 / STEPS)) * top
    return grad_acts, grad_weight


def solution(mesh):
    in_specs = (P("dp", "tensor"), P("dp", "tensor"), P("tensor", None), P())
    out_specs = (P("dp", "tensor"), P(("dp", "tensor"), None))
    return jax.shard_map(body, mesh=mesh, in_specs=in_specs, out_specs=out_specs, check_vma=False)
```

```python
import jax
import jax.numpy as jnp
from jax import lax
from jax.experimental import pallas as pl
from jax.experimental.pallas import tpu as pltpu
from jax.sharding import PartitionSpec as P

NX, NY, NZ = 4, 4, 8
VPASS = 5
LEAD, SLICES = 5, 4
BLK = 128
BF, F32 = jnp.bfloat16, jnp.float32
STEPS = 32767.0
MESH = pl.DeviceIdType.MESH


def kernel(go, acts, weight, mask, own, R, gw, gm, G, A, At, V, K, part, H, S, M,
           t_send, a_send, v_send, w_send, z_send, y_send, b_send, s_send, m_send, r_send,
           t_recv, a_recv, v_recv, w_recv, z_recv, yp_recv, ym_recv, y2_recv,
           yq_recv, yn_recv, y3_recv, b_recv, b2_recv, s_recv, m_recv, h_recv, r_recv, o_recv):
    x = lax.axis_index("dp")
    t = lax.axis_index("tensor")
    y, z, c = t // (2 * NZ), (t % (2 * NZ)) // 2, t % 2
    mine = pl.ds(pl.multiple_of(c * BLK, BLK), BLK)
    other = pl.ds(pl.multiple_of((1 - c) * BLK, BLK), BLK)
    columns = pl.ds(pl.multiple_of(t * 2 * BLK, 2 * BLK), 2 * BLK)
    tokens = go.shape[0]
    half = tokens // 2
    low, high = pl.ds(0, half), pl.ds(half, half)
    mate = y * 2 * NZ + z * 2 + (1 - c)
    up = ((y + 1) % NY) * 2 * NZ + z * 2 + c
    down = ((y + NY - 1) % NY) * 2 * NZ + z * 2 + c
    right = y * 2 * NZ + ((z + 1) % NZ) * 2 + c
    left = y * 2 * NZ + ((z + NZ - 1) % NZ) * 2 + c

    def send(src, dst, send_sem, recv_sem, to_x, to_t):
        pltpu.make_async_remote_copy(
            src_ref=src, dst_ref=dst, send_sem=send_sem, recv_sem=recv_sem,
            device_id=(to_x, to_t), device_id_type=MESH,
        ).start()

    def wait(region, sem):
        pltpu.make_async_copy(region, region, sem).wait()

    def scalar(row, h):
        return mask[x * 2 * NZ + row, 2 * t + h].astype(F32)

    barrier = pltpu.get_barrier_semaphore()
    partner = x * 2 * NZ + z * 2 + c

    @pl.loop(0, NY * 2 * NZ)
    def _(n):
        @pl.when(n != t)
        def _():
            pl.semaphore_signal(barrier, inc=1, device_id=(x, n), device_id_type=MESH)

    @pl.loop(1, NX)
    def _(step):
        @pl.loop(0, 2 * NZ)
        def _(n):
            pl.semaphore_signal(barrier, inc=1, device_id=((x + step) % NX, y * 2 * NZ + n), device_id_type=MESH)

    @pl.when(x != y)
    def _():
        pl.semaphore_signal(barrier, inc=1, device_id=(y, partner), device_id_type=MESH)

    greeted = NY * 2 * NZ - 1 + (NX - 1) * 2 * NZ

    @pl.when(x != y)
    def _():
        pl.semaphore_wait(barrier, greeted + 1)

    @pl.when(x == y)
    def _():
        pl.semaphore_wait(barrier, greeted)


    for part_of, rows in enumerate((low, high)):
        @pl.when(x != y)
        def _():
            send(go.at[rows], G.at[x, 0, rows, mine], t_send, t_recv.at[part_of], y, partner)

        @pl.when(x == y)
        def _():
            pltpu.make_async_copy(go.at[rows], G.at[x, 0, rows, mine], t_recv.at[part_of]).start()

    east, west = (x + 1) % NX, (x + NX - 1) % NX
    pltpu.make_async_copy(acts, A.at[x], a_recv.at[0]).start()

    def start_acts():
        send(acts, A.at[x], a_send, a_recv.at[1], east, t)
        send(acts, A.at[x], a_send, a_recv.at[2], west, t)

    def pass_acts():
        wait(A.at[west], a_recv.at[1])
        piece = A.at[west, pl.ds(0, half)]
        send(piece, piece, a_send, a_recv.at[3], east, t)
        wait(A.at[east], a_recv.at[2])
        piece = A.at[east, pl.ds(half, half)]
        send(piece, piece, a_send, a_recv.at[3], west, t)

    def finish_acts():
        wait(A.at[x], a_recv.at[0])
        wait(A.at[(x + 2) % NX], a_recv.at[3])
        for d in range(NX):
            At[d] = A[d].T

    quarter = BLK // NX
    wide = V.shape[2]
    strip = weight.at[pl.ds(pl.multiple_of(x * quarter, quarter), quarter)]

    def start_weights():
        for step in range(NY):
            there = (y + step) % NY
            src = strip.at[:, pl.ds(pl.multiple_of(there * wide, wide), wide)]
            if step == 0:
                pltpu.make_async_copy(src, V.at[y], v_recv).start()
            else:
                send(src, V.at[y], v_send, v_recv, x, there * 2 * NZ + 2 * z + c)

    def pass_weights():
        wait(V, v_recv)
        dst = K.at[pl.ds(pl.multiple_of(BLK * (2 * z + c) + quarter * x, quarter), quarter)]

        @pl.loop(0, NX * 2 * NZ)
        def _(m):
            e, n = m // (2 * NZ), m % (2 * NZ)
            src = V.at[e, :, pl.ds(pl.multiple_of(n * 2 * BLK, 2 * BLK), 2 * BLK)]
            same = (e == x) & (n == 2 * z + c)

            @pl.when(same)
            def _():
                pltpu.make_async_copy(src, dst, w_recv).start()

            @pl.when(jnp.logical_not(same))
            def _():
                send(src, dst, w_send, w_recv, e, y * 2 * NZ + n)

    def finish_weights():
        wait(K, w_recv)

        @pl.loop(0, 2 * NZ)
        def _(f):
            rows = pl.ds(pl.multiple_of(f * BLK, BLK), BLK)
            for h in range(2):
                cols = slice(h * BLK, (h + 1) * BLK)
                K[rows, cols] = (K[rows, cols].astype(F32) * scalar(f, h)).astype(BF)

    start_weights()

    def chunk(k):
        return (z + NZ + ((k + 1) // 2) * (1 - 2 * (k % 2))) % NZ

    def stage_z(k):
        block = G.at[y, k, :, mine]

        @pl.when(k == 0)
        def _():
            for part_of, rows in enumerate((low, high)):
                piece = G.at[y, k, rows, mine]
                wait(piece, t_recv.at[part_of])
                send(piece, piece, y_send, yp_recv.at[k], x, up)
                send(piece, piece, y_send, ym_recv.at[k], x, down)

        @pl.when(k > 0)
        def _():
            wait(block, z_recv.at[k])

        @pl.when((k == 0) | ((k % 2 == 1) & (k < 7)))
        def _():
            to_k = jnp.where(k == 0, 1, k + 2)
            send(block, G.at[y, to_k, :, mine], z_send, z_recv.at[to_k], x, right)

        @pl.when((k % 2 == 0) & (k < 6))
        def _():
            send(block, G.at[y, k + 2, :, mine], z_send, z_recv.at[k + 2], x, left)

        @pl.when((k > 0) & (k < LEAD))
        def _():
            send(block, block, y_send, yp_recv.at[k], x, up)
            send(block, block, y_send, ym_recv.at[k], x, down)

        send(block, block, b_send, b_recv.at[0, k], x, mate)

    below, above, beyond = (y + NY - 1) % NY, (y + 1) % NY, (y + 2) % NY

    def stage_y(k):
        block = G.at[below, k, :, mine]
        wait(block, yp_recv.at[k])
        piece = G.at[below, k, low, mine]
        send(piece, piece, y_send, y2_recv.at[k], x, up)
        send(block, block, b_send, b_recv.at[1, k], x, mate)
        block = G.at[above, k, :, mine]
        wait(block, ym_recv.at[k])
        piece = G.at[above, k, high, mine]
        send(piece, piece, y_send, y2_recv.at[k], x, down)
        send(block, block, b_send, b_recv.at[2, k], x, mate)

    def stage_far(k):
        block = G.at[beyond, k, :, mine]
        wait(block, y2_recv.at[k])
        send(block, block, b_send, b_recv.at[3, k], x, mate)

    late = pl.ds(LEAD, NZ - LEAD)
    size = tokens // SLICES

    def rows_of(j, part_of=None):
        if part_of is None:
            return pl.ds(pl.multiple_of(j * size, size), size)
        return pl.ds(pl.multiple_of(j * size + part_of * (size // 2), size // 2), size // 2)

    def slice_start(j):
        block = G.at[y, late, rows_of(j), mine]
        send(block, block, y_send, yq_recv.at[j], x, up)
        send(block, block, y_send, yn_recv.at[j], x, down)

    def slice_y(j):
        block = G.at[below, late, rows_of(j), mine]
        wait(block, yq_recv.at[j])
        piece = G.at[below, late, rows_of(j, 0), mine]
        send(piece, piece, y_send, y3_recv.at[j], x, up)
        send(block, block, b_send, b2_recv.at[0, j], x, mate)
        block = G.at[above, late, rows_of(j), mine]
        wait(block, yn_recv.at[j])
        piece = G.at[above, late, rows_of(j, 1), mine]
        send(piece, piece, y_send, y3_recv.at[j], x, down)
        send(block, block, b_send, b2_recv.at[1, j], x, mate)

    def slice_far(j):
        block = G.at[beyond, late, rows_of(j), mine]
        wait(block, y3_recv.at[j])
        send(block, block, b_send, b2_recv.at[2, j], x, mate)

    def slice_input_grad(j):
        for kind, d in enumerate((below, above, beyond)):
            wait(G.at[d, late, rows_of(j), other], b2_recv.at[kind, j])

        @pl.loop(0, NX)
        def _(rel):
            d = (x + 2 + rel) % NX
            rows = rows_of(j)
            total = jnp.zeros((size, 2 * BLK), F32)
            for k in range(NZ):
                kept = K[pl.ds(pl.multiple_of(2 * BLK * chunk(k), 2 * BLK), 2 * BLK)]
                total += jnp.dot(G[d, k, rows], kept, preferred_element_type=F32)
            part[d, rows] = total

            @pl.when(rel == 0)
            def _():
                send(part.at[d, rows_of(j, 0)], H.at[0, j], r_send, h_recv.at[0, j], east, t)
                send(part.at[d, rows_of(j, 1)], H.at[1, j], r_send, h_recv.at[1, j], west, t)

            @pl.when(rel == 1)
            def _():
                send(part.at[d, rows_of(j, 0)], R.at[1, rows_of(j, 0)], r_send, r_recv.at[j], west, t)

            @pl.when(rel == 2)
            def _():
                pltpu.make_async_copy(part.at[d, rows_of(j)], own.at[rows_of(j)], o_recv).start()

            @pl.when(rel == 3)
            def _():
                send(part.at[d, rows_of(j, 1)], R.at[0, rows_of(j, 1)], r_send, r_recv.at[j], east, t)

    def slice_pass(j):
        wait(H.at[0, j], h_recv.at[0, j])
        part[east, rows_of(j, 0)] += H[0, j]
        send(part.at[east, rows_of(j, 0)], R.at[0, rows_of(j, 0)], r_send, r_recv.at[j], east, t)
        wait(H.at[1, j], h_recv.at[1, j])
        part[west, rows_of(j, 1)] += H[1, j]
        send(part.at[west, rows_of(j, 1)], R.at[1, rows_of(j, 1)], r_send, r_recv.at[j], west, t)

    def slice_finish(j):
        wait(R.at[:, rows_of(j)], r_recv.at[j])

    scale_factor = 1.0 / (tokens * NX) ** 0.5

    def stage_weight_grad(k):
        zc = chunk(k)

        @pl.when(k < LEAD)
        def _():
            for kind, d in enumerate((y, below, above, beyond)):
                wait(G.at[d, k, :, other], b_recv.at[kind, k])

        total = jnp.dot(At[0], G[0, k], preferred_element_type=F32)
        for d in range(1, NX):
            total += jnp.dot(At[d], G[d, k], preferred_element_type=F32)
        total = total.T * scale_factor
        for r in range(2):
            for h in range(2):
                tile = total[r * BLK:(r + 1) * BLK, h * BLK:(h + 1) * BLK] * scalar(2 * zc + r, h)
                tile = tile.reshape(4, BLK // 4, BLK)
                top = jnp.max(jnp.abs(tile), axis=1, keepdims=True)
                steps = (tile * jnp.where(top > 0, 1.0 / top, 0.0)) * STEPS
                here = (pl.ds(8 * zc + 4 * r, 4), slice(None), slice(h * BLK, (h + 1) * BLK))
                S[here] = jnp.round(steps).astype(jnp.int16)
                M[here] = top

        @pl.loop(0, 8)
        def _(j):
            n = 8 * zc + j

            @pl.when(n == t)
            def _():
                pltpu.make_async_copy(S.at[n], gw.at[:, columns], s_recv).start()
                pltpu.make_async_copy(M.at[n], gm.at[:, columns], m_recv).start()

            @pl.when(n != t)
            def _():
                send(S.at[n], gw.at[:, columns], s_send, s_recv, x, n)
                send(M.at[n], gm.at[:, columns], m_send, m_recv, x, n)

    @pl.loop(0, LEAD + 4)
    def _(i):
        @pl.when(i < NZ)
        def _():
            stage_z(i)

        @pl.when((i >= 2) & (i < LEAD + 2))
        def _():
            stage_y(i - 2)

        @pl.when(i == LEAD + 2)
        def _():
            pl.loop(0, SLICES)(slice_start)

        @pl.when((i >= 3) & (i < LEAD + 3))
        def _():
            stage_far(i - 3)

        @pl.when(i == 0)
        def _():
            start_acts()

        @pl.when(i == 2)
        def _():
            pass_acts()

        @pl.when(i == VPASS)
        def _():
            pass_weights()

        @pl.when(i == 4)
        def _():
            finish_acts()

        @pl.when(i >= 4)
        def _():
            stage_weight_grad(i - 4)

    @pl.loop(0, SLICES + 2)
    def _(i):
        @pl.when(i < SLICES)
        def _():
            slice_y(i)

        @pl.when((i >= 1) & (i < SLICES + 1))
        def _():
            slice_far(i - 1)

        @pl.when(i == 2)
        def _():
            finish_weights()

            @pl.loop(LEAD, NZ)
            def _(k):
                wait(G.at[y, k, :, other], b_recv.at[0, k])

        @pl.when((i >= 2) & (i < SLICES + 2))
        def _():
            slice_input_grad(i - 2)

        @pl.when((i >= 3) & (i < SLICES + 2))
        def _():
            slice_pass(i - 3)

        @pl.when(i == SLICES + 1)
        def _():
            pl.loop(LEAD, NZ)(stage_weight_grad)

    slice_pass(SLICES - 1)
    pl.loop(0, SLICES)(slice_finish)
    wait(gw, s_recv)
    wait(gm, m_recv)
    wait(own, o_recv)

    @pl.when(x != y)
    def _():
        wait(go, t_send)

    wait(V.at[pl.ds(0, 3)], v_send)
    wait(K.at[pl.ds(0, 63 * quarter)], w_send)

    wait(A.at[pl.ds(0, 3)], a_send)
    wait(G.at[0, pl.ds(0, 7), :, pl.ds(0, BLK)], z_send)
    wait(G.at[pl.ds(0, 3), pl.ds(0, 4)], y_send)
    wait(G.at[pl.ds(0, 2)], b_send)
    wait(S.at[pl.ds(0, 63)], s_send)
    wait(M.at[pl.ds(0, 63)], m_send)
    wait(part.at[pl.ds(0, 3)], r_send)


def body(grad_out, acts, weight, block_mask):
    tokens, d_tile = grad_out.shape
    ff_tile = acts.shape[1]
    full_width = weight.shape[1]
    dma = pltpu.SemaphoreType.DMA
    own, sums, steps, top = pl.pallas_call(
        kernel,
        out_shape=(
            jax.ShapeDtypeStruct((tokens, ff_tile), F32),
            jax.ShapeDtypeStruct((2, tokens, ff_tile), F32),
            jax.ShapeDtypeStruct((d_tile // NX, full_width), jnp.int16),
            jax.ShapeDtypeStruct((1, full_width), F32),
        ),
        in_specs=[pl.BlockSpec(memory_space=pltpu.HBM)] * 3 + [pl.BlockSpec(memory_space=pltpu.SMEM)],
        out_specs=[pl.BlockSpec(memory_space=pltpu.HBM)] * 4,
        scratch_shapes=[
            pltpu.VMEM((NX, NZ, tokens, 2 * BLK), BF),
            pltpu.VMEM((NX, tokens, ff_tile), BF),
            pltpu.VMEM((NX, ff_tile, tokens), BF),
            pltpu.VMEM((NY, d_tile // NX, full_width // NY), BF),
            pltpu.VMEM((2 * NZ * BLK, ff_tile), BF),
            pltpu.VMEM((NX, tokens, ff_tile), F32),
            pltpu.VMEM((2, SLICES, tokens // SLICES // 2, ff_tile), F32),
            pltpu.VMEM((8 * NZ, BLK // NX, ff_tile), jnp.int16),
            pltpu.VMEM((8 * NZ, 1, ff_tile), F32),
        ] + [dma] * 10 + [dma((2,)), dma((4,)), dma, dma] + [dma((NZ,))] + [dma((LEAD,))] * 3 + [dma((SLICES,))] * 3
        + [dma((4, NZ)), dma((3, SLICES)), dma, dma, dma((2, SLICES)), dma((SLICES,)), dma],
        compiler_params=pltpu.CompilerParams(
            collective_id=0, has_side_effects=True, vmem_limit_bytes=63 * 1024 * 1024
        ),
    )(grad_out, acts, weight, block_mask)
    grad_acts = (own + sums[0] + sums[1]).astype(BF)
    grad_weight = (steps.astype(F32) * (1.0 / STEPS)) * top
    return grad_acts, grad_weight


def solution(mesh):
    in_specs = (P("dp", "tensor"), P("dp", "tensor"), P("tensor", None), P())
    out_specs = (P("dp", "tensor"), P(("dp", "tensor"), None))
    return jax.shard_map(body, mesh=mesh, in_specs=in_specs, out_specs=out_specs, check_vma=False)
```
